256 devices in a mesh: row: 64 (over z, y, core), col: 4 (over x).
Axes of the slice: x: 4, y: 4, z: 8, core: 2. Of those that a mesh axis runs over, the one named last changes fastest.
Arguments:
- panel_block: float32 [131072, 128], P('row', 'col'), may hold values from -6 to 6
- trailing: float32 [131072, 2048], P('row', 'col'), may hold values from -6 to 6
Outputs:
- updated: float32 [131072, 2048], P('row', 'col')
- reflectors: float32 [131072, 128], P('row', 'col')
- panel_factor: float32 [128, 128], replicated
The draws below stay inside these ranges and needn't reach their ends.
All inputs are finite; a program needn't handle non-finite values.
Results may differ from the reference program's by a relative error of at most 0.0003.
Values sent between devices are 32-bit elements; how exact they have to be, the bound alone decides.
A program may use at most 64 MiB of HBM per device.

```python
import jax
import jax.numpy as jnp
from jax import lax

B = 128
M = 131072
NC = 2048


def block_scale(rng, shape, pieces, smallest, largest):
    def one(position, parts):
        heights = jax.random.uniform(jax.random.fold_in(jax.random.fold_in(rng, 6), position), (parts,), jnp.float32, smallest / len(pieces), largest / len(pieces))
        return jnp.repeat(jnp.exp(heights), shape[position] // parts).reshape((-1,) + (1,) * (len(shape) - position - 1))

    factor_of = one(*pieces[0])
    for cut in pieces[1:]:
        factor_of = factor_of * one(*cut)
    return factor_of


def scatter_about(key, shape, scale, bound, split=(), held_as=jnp.bfloat16):
    array = jax.random.normal(key, shape, jnp.float32) * scale
    if len(split) > 0:
        array = block_scale(key, shape, split, -0.22, 0.18) * array
    return jnp.clip(array, min=-bound, max=bound).astype(held_as)


def setup_inputs(seed: int = 0) -> dict:
    keys = jax.random.split(jax.random.key(seed), 3)
    return {
        "panel_block": scatter_about(keys[0], (M, B), 1.0, 6.0, ((0, 64), (1, 4)), jnp.float32),
        "trailing": scatter_about(keys[1], (M, NC), 1.0, 6.0, ((0, 64), (1, 4)), jnp.float32),
    }


HIGH = lax.Precision.HIGHEST

def decompose(matrix):
    extent = matrix.shape[0]
    positions = jnp.arange(extent)

    def advance(column, current):
        row_pick = lax.dynamic_index_in_dim(current, column, 0, keepdims=False)
        col_pick = lax.dynamic_index_in_dim(current, column, 1, keepdims=False)
        pivot_value = lax.dynamic_index_in_dim(row_pick, column, 0, keepdims=False)
        below_mask = positions > column
        factor_col = jnp.where(below_mask, col_pick / pivot_value, jnp.float32(0.0))
        current = current - factor_col[:, None] * jnp.where(below_mask, row_pick, jnp.float32(0.0))[None, :]
        place_mask = (positions == column)[None, :] & below_mask[:, None]
        return jnp.where(place_mask, factor_col[:, None], current)
    return lax.fori_loop(0, extent, advance, matrix)

def reference(panel_block, trailing):
    width = panel_block.shape[1]
    gram_full = lax.dot_general(panel_block.astype(jnp.float32), panel_block.astype(jnp.float32), (((0,), (0,)), ((), ())), precision=HIGH, preferred_element_type=jnp.float32)
    factor = jnp.linalg.cholesky(gram_full).T
    q_trans = jax.scipy.linalg.solve_triangular(factor.T, panel_block.T, lower=True)
    leading = q_trans[:, :width].T
    sign_flip = jnp.where(jnp.diag(leading) >= 0, jnp.float32(-1.0), jnp.float32(1.0))
    packed_lu = decompose(leading - jnp.diag(sign_flip))
    lower_f = jnp.tril(packed_lu, -1) + jnp.eye(width, dtype=jnp.float32)
    upper_f = jnp.triu(packed_lu)
    reflect_t = jax.scipy.linalg.solve_triangular(upper_f.T, q_trans, lower=True)
    reflect_t = reflect_t.at[:, :width].set(lower_f.T)
    coupling_t = jax.scipy.linalg.solve_triangular(lower_f, -(sign_flip[:, None] * upper_f.T), lower=True, unit_diagonal=True)
    products = lax.dot_general(trailing.astype(jnp.float32), reflect_t.astype(jnp.float32), (((0,), (1,)), ((), ())), precision=HIGH, preferred_element_type=jnp.float32)
    mixed = lax.dot_general(products.astype(jnp.float32), coupling_t.astype(jnp.float32), (((1,), (1,)), ((), ())), precision=HIGH, preferred_element_type=jnp.float32)
    change = lax.dot_general(reflect_t.astype(jnp.float32), mixed.astype(jnp.float32), (((0,), (1,)), ((), ())), precision=HIGH, preferred_element_type=jnp.float32)
    updated = trailing - change
    return (updated, reflect_t.T, sign_flip[:, None] * factor)
```

```python
import functools

import jax
import jax.numpy as jnp
from jax import lax
from jax.experimental import pallas as pl
from jax.experimental.pallas import tpu as pltpu
from jax.sharding import PartitionSpec as P

F32 = jnp.float32
BF16 = jnp.bfloat16
HIGH = lax.Precision.HIGHEST
N = 128
Q = 8


def dot(a, b, dims=((1,), (0,)), precision=None):
    return lax.dot_general(a, b, (dims, ((), ())), precision=precision, preferred_element_type=F32)


def split(x):
    hi = x.astype(BF16)
    return hi, (x - hi.astype(F32)).astype(BF16)


def eliminate(m_ref, b, bottom):
    r0 = 8 * b
    lane = lax.broadcasted_iota(jnp.int32, (8, N), 1)
    sub = lax.broadcasted_iota(jnp.int32, (8, N), 0)
    parts = []
    if r0 + 8 < N:
        parts.append((r0 + 8, N - r0 - 8, False))
    if bottom:
        parts.append((N, r0 + 8, True))
    rows = m_ref[r0 : r0 + 8, :]
    rest = [m_ref[s : s + n, :] for s, n, _ in parts]
    cols = [
        [jnp.broadcast_to(p[:, r0 + j : r0 + j + 1], (p.shape[0], N)) for j in range(8)]
        for p in [rows] + rest
    ]
    mults, pivots = [], None
    for k in range(8):
        c0 = cols[0][k]
        d = jnp.broadcast_to(c0[k : k + 1, :], (8, N))
        inv = 1.0 / d
        pivots = d if pivots is None else jnp.where(sub == k, d, pivots)
        ms = [jnp.where(sub > k, c0 * inv, 0.0)] + [c[k] * inv[0:1, :] for c in cols[1:]]
        mults.append(ms)
        for j in range(k + 1, 8):
            top = cols[0][j][k : k + 1, :]
            for i in range(len(cols)):
                cols[i][j] = cols[i][j] - ms[i] * top
    pivot_rows = []
    for k in range(8):
        lk = r0 + k
        row = jnp.where(lane[0:1] == lk, 1.0, rows[k : k + 1, :])
        rows = jnp.where((lane == lk) & (sub > k), 0.0, rows) - mults[k][0] * row
        pivot_rows.append(jnp.where((lane[0:1] > lk) & (lane[0:1] < r0 + 8), 0.0, row))
    for i, (s, n, low) in enumerate(parts):
        lane_n = lax.broadcasted_iota(jnp.int32, (n, N), 1)
        acc = jnp.where((lane_n >= r0) & (lane_n < r0 + 8), 0.0, rest[i])
        for k in range(8):
            row = jnp.where(lane[0:1] >= r0 + 8, pivot_rows[k], 0.0) if low else pivot_rows[k]
            acc = acc - mults[k][i + 1] * row
        if low:
            for k in range(8):
                acc = jnp.where(lane_n == r0 + k, mults[k][i + 1], acc)
        m_ref[s : s + n, :] = acc
    m_ref[r0 : r0 + 8, :] = rows
    return pivots


def remote(src, dst, send, recv, device):
    return pltpu.make_async_remote_copy(
        src_ref=src, dst_ref=dst, send_sem=send, recv_sem=recv, device_id=device, device_id_type=pl.DeviceIdType.MESH
    )


def factor_kernel(
    nz, nx,
    pt_ref, t_ref,
    ahi_out, alo_out, k_out, d_out, vxt_out, l1xt_out, r_out,
    at, t, thi, tlo, a1t, t1, g, grs, gz, c, crs, cz, m1, m2, rit, bmat, gsum, csum,
    load_sem, xs, xr, gs1, gr1, gs2, gr2, gs3, gr3, cs1, cr1, cs2, cr2, cs3, cr3, ts1, tr1, ts2, tr2, ts3, tr3,
    as1, ar1, as2, ar2, as3, ar3,
):
    r = lax.axis_index("row")
    x = lax.axis_index("col")
    z, q = lax.div(r, Q), lax.rem(r, Q)
    half = pt_ref.shape[1] // 2
    w = N // nx
    xp, xm = lax.rem(x + 1, nx), lax.rem(x + nx - 1, nx)

    def at_q(o):
        return {"row": z * Q + lax.rem(q + o, Q)}

    def at_z(o):
        return {"row": lax.rem(z + o, nz) * Q + q}

    own = pl.multiple_of(x * w, w)
    load_t = pltpu.make_async_copy(t_ref, t, load_sem.at[0])
    load_t.start()
    load_a = pltpu.make_async_copy(pt_ref, at.at[pl.ds(own, w), :], load_sem.at[1])
    load_a.start()

    barrier = pltpu.get_barrier_semaphore()
    for o in range(1, Q):
        pl.semaphore_signal(barrier, inc=1, device_id=at_q(o), device_id_type=pl.DeviceIdType.MESH)
    for o in range(1, nz):
        pl.semaphore_signal(barrier, inc=1, device_id=at_z(o), device_id_type=pl.DeviceIdType.MESH)
    for o in range(1, nx):
        pl.semaphore_signal(
            barrier, inc=1, device_id={"col": lax.rem(x + o, nx)}, device_id_type=pl.DeviceIdType.MESH
        )
    pl.semaphore_wait(barrier, Q - 1 + nz - 1 + nx - 1)

    mine = at.at[pl.ds(own, w), :]
    h0, h1 = pl.ds(0, half), pl.ds(half, half)

    def strip(owner, h):
        return at.at[pl.ds(pl.multiple_of(owner * w, w), w), h]

    plus = [remote(pt_ref.at[:, h], strip(x, h), xs.at[i], xr.at[i], {"col": xp}) for i, h in enumerate((h0, h1))]
    minus = [
        remote(pt_ref.at[:, h], strip(x, h), xs.at[3 + i], xr.at[3 + i], {"col": xm}) for i, h in enumerate((h1, h0))
    ]
    for a, b in zip(plus, minus):
        a.start()
        b.start()

    root = r == 0
    first = z == 0
    piece = N // Q
    mine_piece = pl.ds(pl.multiple_of(q * piece, piece), piece)

    def t1_to_q(o):
        rows = pl.ds(pl.multiple_of(lax.rem(q + o, Q) * piece, piece), piece)
        return remote(t_ref.at[rows, :], t1.at[rows, :], ts1.at[o], tr1.at[0], at_q(o))

    def a1_to_q(o):
        return remote(pt_ref.at[:, pl.ds(0, N)], a1t.at[pl.ds(own, w), :], as1.at[o], ar1.at[0], at_q(o))

    def t1_to_z(o):
        return remote(t1.at[mine_piece, :], t1.at[mine_piece, :], ts2.at[o], tr2.at[0], at_z(o))

    def a1_to_z(o):
        return remote(a1t.at[pl.ds(own, w), :], a1t.at[pl.ds(own, w), :], as2.at[o], ar2.at[0], at_z(o))

    def t1_gather(o):
        return remote(t1.at[mine_piece, :], t1.at[mine_piece, :], ts3.at[o], tr3.at[o], at_q(o))

    def a1_gather(o):
        rows = a1t.at[pl.ds(own, w), :]
        return remote(rows, rows, as3.at[o], ar3.at[o], {"col": lax.rem(x + o, nx)})

    @pl.when(root)
    def _():
        for o in range(1, Q):
            a1_to_q(o).start()
        for o in range(1, Q):
            t1_to_q(o).start()
        one = pltpu.make_async_copy(t_ref.at[mine_piece, :], t1.at[mine_piece, :], load_sem.at[2])
        two = pltpu.make_async_copy(pt_ref.at[:, pl.ds(0, N)], a1t.at[pl.ds(own, w), :], load_sem.at[3])
        one.start()
        two.start()
        one.wait()
        two.wait()

    @pl.when(first & jnp.logical_not(root))
    def _():
        a1_to_q(1).wait_recv()
        t1_to_q(1).wait_recv()

    @pl.when(first)
    def _():
        for o in range(1, nz):
            a1_to_z(o).start()
        for o in range(1, nz):
            t1_to_z(o).start()

    @pl.when(jnp.logical_not(first))
    def _():
        a1_to_z(1).wait_recv()
        t1_to_z(1).wait_recv()

    for o in range(1, nx):
        a1_gather(o).start()
    for o in range(1, Q):
        t1_gather(o).start()

    load_t.wait()
    thi[...] = t[...].astype(BF16)
    tlo[...] = (t[...] - thi[...].astype(F32)).astype(BF16)
    load_a.wait()

    plus[0].wait_recv()
    far_plus = remote(strip(xm, h0), strip(xm, h0), xs.at[2], xr.at[2], {"col": xp})
    far_plus.start()
    minus[0].wait_recv()
    far_minus = remote(strip(xp, h1), strip(xp, h1), xs.at[5], xr.at[5], {"col": xm})
    far_minus.start()
    plus[1].wait_recv()
    minus[1].wait_recv()
    far_plus.wait_recv()
    far_minus.wait_recv()

    g[...] = dot(at[...], at[...], ((1,), (1,)), HIGH)

    def scatter(src, dst, ss, rs):
        out = []
        for o in range(1, Q):
            rows = pl.ds(pl.multiple_of(lax.rem(q + o, Q) * piece, piece), piece)
            out.append(remote(src.at[rows, :], dst.at[o], ss.at[o], rs.at[o], at_q(o)))
        return out

    def exchange(buf, ss, rs):
        return [remote(buf.at[z], buf.at[z], ss.at[o], rs.at[o], at_z(o)) for o in range(1, nz)]

    def gather(buf, ss, rs):
        return [remote(buf.at[mine_piece, :], buf.at[mine_piece, :], ss.at[o], rs.at[o], at_q(o)) for o in range(1, Q)]

    def start(copies):
        for copy in copies:
            copy.start()

    def arrive(copies):
        for copy in copies:
            copy.wait_recv()

    def sent(copies):
        for copy in copies:
            copy.wait_send()

    g1, g2, g3 = scatter(g, grs, gs1, gr1), exchange(gz, gs2, gr2), gather(gsum, gs3, gr3)
    c1, c2, c3 = scatter(c, crs, cs1, cr1), exchange(cz, cs2, cr2), gather(csum, cs3, cr3)

    def sum_scattered(src, slots, buf):
        total = src[mine_piece, :]
        for o in range(1, Q):
            total = total + slots[o]
        buf[z] = total

    def sum_exchanged(buf, dst):
        total = buf[0]
        for o in range(1, nz):
            total = total + buf[o]
        dst[mine_piece, :] = total

    start(g1)
    athi, atlo = split(at[...])
    both = jnp.concatenate([athi, atlo], axis=0)
    high = dot(both, thi[...])
    c[...] = high[:N] + high[N:] + dot(athi, tlo[...])
    arrive(g1)
    sum_scattered(g, grs, gz)
    start(g2)
    start(c1)
    for i in range(0, at.shape[1], N):
        hi, lo = split(at[:, i : i + N].T)
        ahi_out[i : i + N, :] = hi
        alo_out[i : i + N, :] = lo
    arrive(g2)
    sent(g1)
    sum_exchanged(gz, gsum)
    start(g3)
    arrive([a1_gather(o) for o in range(1, nx)])
    a1 = a1t[...].T
    arrive(g3)
    sent(g3)

    lane = lax.broadcasted_iota(jnp.int32, (8, N), 1)
    sub = lax.broadcasted_iota(jnp.int32, (8, N), 0)
    m1[...] = gsum[...]
    for b in range(N // 8):
        if b == 4:
            arrive(c1)
            sum_scattered(c, crs, cz)
            start(c2)
        if b == 12:
            arrive(c2)
            sent(c1)
            sum_exchanged(cz, csum)
            start(c3)
        rows = slice(8 * b, 8 * b + 8)
        pivots = eliminate(m1, b, False)
        scale = lax.rsqrt(pivots)
        row = sub + 8 * b
        block = m1[rows, :] * scale
        upper = jnp.where(lane >= row, block, 0.0)
        inverse = jnp.where(lane < row, block, jnp.where(lane == row, scale, 0.0))
        lead = a1[rows, :]
        diag = jnp.sum(lead * inverse, axis=1, keepdims=True)
        sign = jnp.where(diag >= 0, -1.0, 1.0)
        signed = sign * upper
        r_out[rows, :] = signed
        rit[rows, :] = sign * inverse
        m2[rows, :] = lead - signed
    row = lax.broadcasted_iota(jnp.int32, (N, N), 0)
    col = lax.broadcasted_iota(jnp.int32, (N, N), 1)
    bmat[...] = m2[0:N, :]
    m2[N : 2 * N, :] = jnp.where(row == col, 1.0, 0.0)
    for b in range(N // 8):
        eliminate(m2, b, True)
    v = jnp.where(row <= col, m2[N : 2 * N, :], 0.0)
    linv = jnp.where(row == col, 1.0, jnp.where(row > col, m2[0:N, :], 0.0))
    vt = v.T
    m1[...] = vt
    vxt_out[...] = m1[pl.ds(own, w), :]
    l1t = jnp.where(row == col, 1.0, jnp.where(row < col, dot(vt, bmat[...], ((1,), (1,)), HIGH), 0.0))
    m1[...] = l1t
    l1xt_out[...] = m1[pl.ds(own, w), :]
    arrive(c3)
    arrive([t1_gather(o) for o in range(1, Q)])
    d = dot(rit[...], csum[...], precision=HIGH)
    d_out[...] = d
    k_out[...] = dot(v, dot(linv, t1[...] - d, precision=HIGH), precision=HIGH)

    sent(plus + minus + [far_plus, far_minus])
    sent(g2 + c2 + c3)
    sent([t1_gather(o) for o in range(1, Q)])
    sent([a1_gather(o) for o in range(1, nx)])

    @pl.when(root)
    def _():
        sent([t1_to_q(o) for o in range(1, Q)])
        sent([a1_to_q(o) for o in range(1, Q)])

    @pl.when(first)
    def _():
        sent([t1_to_z(o) for o in range(1, nz)])
        sent([a1_to_z(o) for o in range(1, nz)])


def update_kernel(t_ref, ahi_ref, alo_ref, k_ref, d_ref, vxt_ref, l1xt_ref, out_ref, yt_ref):
    ahi, alo = ahi_ref[...], alo_ref[...]
    khi, klo = split(k_ref[...])
    a2 = jnp.concatenate([ahi, alo], axis=1)
    k2 = jnp.concatenate([khi, khi], axis=0)
    out_ref[...] = t_ref[...] - (dot(a2, k2) + dot(ahi, klo))
    vhi, vlo = split(vxt_ref[...])
    nt = ((1,), (1,))
    yt_ref[...] = dot(vhi, ahi, nt) + dot(vhi, alo, nt) + dot(vlo, ahi, nt)

    @pl.when((lax.axis_index("row") == 0) & (pl.program_id(0) == 0))
    def _():
        out_ref[0:N, :] = d_ref[...]
        yt_ref[:, 0:N] = l1xt_ref[...]


def per_device(nz, nx, panel_block, trailing):
    rows, cols = trailing.shape
    w = N // nx
    dma = pltpu.SemaphoreType.DMA
    any_spec = pl.BlockSpec(memory_space=pl.ANY)
    vmem = pl.BlockSpec(memory_space=pltpu.VMEM)
    shape = jax.ShapeDtypeStruct
    ahi, alo, k, d, vxt, l1xt, factor = pl.pallas_call(
        functools.partial(factor_kernel, nz, nx),
        out_shape=[
            shape((rows, N), BF16), shape((rows, N), BF16), shape((N, cols), F32), shape((N, cols), F32),
            shape((w, N), F32), shape((w, N), F32), shape((N, N), F32),
        ],
        in_specs=[any_spec, any_spec],
        out_specs=[vmem] * 7,
        scratch_shapes=[
            pltpu.VMEM((N, rows), F32), pltpu.VMEM((rows, cols), F32), pltpu.VMEM((rows, cols), BF16),
            pltpu.VMEM((rows, cols), BF16), pltpu.VMEM((N, N), F32), pltpu.VMEM((N, cols), F32),
            pltpu.VMEM((N, N), F32), pltpu.VMEM((Q, N // Q, N), F32), pltpu.VMEM((nz, N // Q, N), F32),
            pltpu.VMEM((N, cols), F32), pltpu.VMEM((Q, N // Q, cols), F32), pltpu.VMEM((nz, N // Q, cols), F32),
            pltpu.VMEM((N, N), F32), pltpu.VMEM((2 * N, N), F32), pltpu.VMEM((N, N), F32), pltpu.VMEM((N, N), F32),
            pltpu.VMEM((N, N), F32), pltpu.VMEM((N, cols), F32),
            dma((4,)), dma((6,)), dma((6,)),
        ] + [dma((8,))] * 12 + [
            dma((8,)), dma((1,)), dma((8,)), dma((1,)), dma((8,)), dma((8,)),
            dma((8,)), dma((1,)), dma((8,)), dma((1,)), dma((nx,)), dma((nx,)),
        ],
        compiler_params=pltpu.CompilerParams(
            collective_id=0, has_side_effects=True, vmem_limit_bytes=48 * 1024 * 1024
        ),
        name="factor",
    )(panel_block.T, trailing)
    tile = 512
    updated, yt = pl.pallas_call(
        update_kernel,
        grid=(rows // tile,),
        out_shape=[shape((rows, cols), F32), shape((w, rows), F32)],
        in_specs=[
            pl.BlockSpec((tile, cols), lambda i: (i, 0)), pl.BlockSpec((tile, N), lambda i: (i, 0)),
            pl.BlockSpec((tile, N), lambda i: (i, 0)), pl.BlockSpec((N, cols), lambda i: (0, 0)),
            pl.BlockSpec((N, cols), lambda i: (0, 0)), pl.BlockSpec((w, N), lambda i: (0, 0)),
            pl.BlockSpec((w, N), lambda i: (0, 0)),
        ],
        out_specs=[pl.BlockSpec((tile, cols), lambda i: (i, 0)), pl.BlockSpec((w, tile), lambda i: (0, i))],
        compiler_params=pltpu.CompilerParams(vmem_limit_bytes=32 * 1024 * 1024),
        name="update",
    )(trailing, ahi, alo, k, d, vxt, l1xt)
    return updated, yt.T, factor


def solution(mesh):
    nz, nx = mesh.shape["row"] // Q, mesh.shape["col"]
    in_specs = (P("row", "col"), P("row", "col"))
    out_specs = (P("row", "col"), P("row", "col"), P())
    return jax.shard_map(
        functools.partial(per_device, nz, nx), mesh=mesh, in_specs=in_specs, out_specs=out_specs, check_vma=False
    )
```

```python
import functools

import jax
import jax.numpy as jnp
from jax import lax
from jax.experimental import pallas as pl
from jax.experimental.pallas import tpu as pltpu
from jax.sharding import PartitionSpec as P

F32 = jnp.float32
BF16 = jnp.bfloat16
HIGH = lax.Precision.HIGHEST
N = 128
Q = 8


def dot(a, b, dims=((1,), (0,)), precision=None):
    return lax.dot_general(a, b, (dims, ((), ())), precision=precision, preferred_element_type=F32)


def split(x):
    hi = x.astype(BF16)
    return hi, (x - hi.astype(F32)).astype(BF16)


def eliminate(m_ref, b, bottom, out):
    r0 = 8 * b
    lane = lax.broadcasted_iota(jnp.int32, (8, N), 1)
    sub = lax.broadcasted_iota(jnp.int32, (8, N), 0)
    parts = []
    if r0 + 8 < N:
        parts.append((r0 + 8, N - r0 - 8, False))
    if bottom:
        parts.append((N, r0 + 8, True))
    rows = m_ref[r0 : r0 + 8, :]
    rest = [m_ref[s : s + n, :] for s, n, _ in parts]
    cols = [
        [jnp.broadcast_to(p[:, r0 + j : r0 + j + 1], (p.shape[0], N)) for j in range(8)]
        for p in [rows] + rest
    ]
    mults, pivots = [], None
    for k in range(8):
        yield
        c0 = cols[0][k]
        d = jnp.broadcast_to(c0[k : k + 1, :], (8, N))
        inv = 1.0 / d
        pivots = d if pivots is None else jnp.where(sub == k, d, pivots)
        ms = [jnp.where(sub > k, c0 * inv, 0.0)] + [c[k] * inv[0:1, :] for c in cols[1:]]
        mults.append(ms)
        for j in range(k + 1, 8):
            top = cols[0][j][k : k + 1, :]
            for i in range(len(cols)):
                cols[i][j] = cols[i][j] - ms[i] * top
    pivot_rows = []
    for k in range(8):
        lk = r0 + k
        row = jnp.where(lane[0:1] == lk, 1.0, rows[k : k + 1, :])
        rows = jnp.where((lane == lk) & (sub > k), 0.0, rows) - mults[k][0] * row
        pivot_rows.append(jnp.where((lane[0:1] > lk) & (lane[0:1] < r0 + 8), 0.0, row))
    for i, (s, n, low) in enumerate(parts):
        lane_n = lax.broadcasted_iota(jnp.int32, (n, N), 1)
        acc = jnp.where((lane_n >= r0) & (lane_n < r0 + 8), 0.0, rest[i])
        for k in range(8):
            row = jnp.where(lane[0:1] >= r0 + 8, pivot_rows[k], 0.0) if low else pivot_rows[k]
            acc = acc - mults[k][i + 1] * row
        if low:
            for k in range(8):
                acc = jnp.where(lane_n == r0 + k, mults[k][i + 1], acc)
        m_ref[s : s + n, :] = acc
    m_ref[r0 : r0 + 8, :] = rows
    out.append(pivots)


def interleave(*steps):
    steps = list(steps)
    while steps:
        for step in list(steps):
            if next(step, True) is True:
                steps.remove(step)


def remote(src, dst, send, recv, device):
    return pltpu.make_async_remote_copy(
        src_ref=src, dst_ref=dst, send_sem=send, recv_sem=recv, device_id=device, device_id_type=pl.DeviceIdType.MESH
    )


def factor_kernel(
    nz, nx,
    pt_ref, t_ref,
    ahi_out, alo_out, k_out, d_out, vxt_out, l1xt_out, r_out,
    at, t, thi, tlo, a1t, t1, g, gslots, gz, gsum, c, cslots, cz, csum, m1, m2, rit, bmat,
    load_sem, xs, xr, gs1, gr1, gs2, gr2, gs3, gr3, cs1, cr1, cs2, cr2, cs3, cr3, ts1, tr1, ts2, tr2, ts3, tr3,
    as1, ar1, as2, ar2, as3, ar3,
):
    r = lax.axis_index("row")
    x = lax.axis_index("col")
    z, q = lax.div(r, Q), lax.rem(r, Q)
    ny = Q // 2
    y, core = lax.div(q, 2), lax.rem(q, 2)
    w = N // nx
    seg = pt_ref.shape[1] // nx

    def along_x(o):
        return lax.rem(x + o, nx)

    def along_y(o):
        return lax.rem(y + o, ny)

    def at_x(o):
        return {"col": along_x(o)}

    def at_q(o):
        return {"row": z * Q + lax.rem(q + o, Q)}

    def at_z(o):
        return {"row": lax.rem(z + o, nz) * Q + q}

    def at_xy(o):
        return {"row": z * Q + along_y(o % ny) * 2 + core, "col": along_x(o // ny)}

    def at_zc(o):
        return {"row": lax.rem(z + o // 2, nz) * Q + y * 2 + lax.rem(core + o % 2, 2)}

    load_t = pltpu.make_async_copy(t_ref, t, load_sem.at[0])
    load_t.start()
    own = pl.ds(pl.multiple_of(x * w, w), w)
    load_a = pltpu.make_async_copy(pt_ref, at.at[own, :], load_sem.at[1])
    load_a.start()

    barrier = pltpu.get_barrier_semaphore()
    greeted = [at_xy(o) for o in range(1, nx * ny)] + [at_zc(o) for o in range(1, 2 * nz)]
    greeted += [{"row": z * Q + along_y(o) * 2 + (1 - core)} for o in range(1, ny)]
    for device in greeted:
        pl.semaphore_signal(barrier, inc=1, device_id=device, device_id_type=pl.DeviceIdType.MESH)
    pl.semaphore_wait(barrier, len(greeted))

    def columns(s):
        return pl.ds(pl.multiple_of(s * seg, seg), seg)

    def strip(owner, cols):
        return at.at[pl.ds(pl.multiple_of(owner * w, w), w), cols]

    def tell(i, o, s):
        return remote(pt_ref.at[:, columns(s)], strip(x, columns(s)), xs.at[i], xr.at[i], at_x(o))

    def forward(i, o, owner, cols):
        return remote(strip(owner, cols), strip(owner, cols), xs.at[i], xr.at[i], at_x(o))

    xp, xm, x2 = along_x(1), along_x(nx - 1), along_x(2)
    plus, minus = 1, nx - 1
    first_half = pl.ds(pl.multiple_of(xm * seg, seg), seg // 2)
    second_half = pl.ds(pl.multiple_of(xp * seg + seg // 2, seg // 2), seg // 2)
    near_first = [tell(0, plus, xp), tell(1, minus, xm), tell(2, 2, x2)]
    near_rest = [
        tell(3, plus, x), tell(4, minus, x), tell(5, plus, x2), tell(6, minus, x2), tell(7, plus, xm), tell(8, minus, xp),
    ]
    onward = [
        forward(9, plus, xm, columns(x)), forward(10, minus, xp, columns(x)),
        forward(11, plus, xm, first_half), forward(12, minus, xp, second_half),
    ]

    def start(copies):
        for copy in copies:
            copy.start()

    def arrive(copies):
        for copy in copies:
            copy.wait_recv()

    def sent(copies):
        for copy in copies:
            copy.wait_send()

    start(near_first)

    root = r == 0
    first = z == 0
    piece = N // Q
    mine_piece = pl.ds(pl.multiple_of(q * piece, piece), piece)
    lead_cols = pl.ds(0, N)

    def t1_to_q(o):
        rows = pl.ds(pl.multiple_of(lax.rem(q + o, Q) * piece, piece), piece)
        return remote(t_ref.at[rows, :], t1.at[rows, :], ts1.at[o], tr1.at[0], at_q(o))

    def a1_to_q(o):
        return remote(pt_ref.at[:, lead_cols], a1t.at[own, :], as1.at[o], ar1.at[0], at_q(o))

    def t1_to_z(o):
        return remote(t1.at[mine_piece, :], t1.at[mine_piece, :], ts2.at[o], tr2.at[0], at_z(o))

    def a1_to_z(o):
        return remote(a1t.at[own, :], a1t.at[own, :], as2.at[o], ar2.at[0], at_z(o))

    t1_gather = [
        remote(t1.at[mine_piece, :], t1.at[mine_piece, :], ts3.at[o], tr3.at[o], at_q(o)) for o in range(1, Q)
    ]
    a1_gather = [remote(a1t.at[own, :], a1t.at[own, :], as3.at[o], ar3.at[o], at_x(o)) for o in range(1, nx)]
    lead_t = pltpu.make_async_copy(t_ref.at[mine_piece, :], t1.at[mine_piece, :], load_sem.at[2])
    lead_a = pltpu.make_async_copy(pt_ref.at[:, lead_cols], a1t.at[own, :], load_sem.at[3])

    @pl.when(root)
    def _():
        for o in range(1, Q):
            a1_to_q(o).start()
        lead_a.start()
        lead_t.start()
        for o in range(1, Q):
            t1_to_q(o).start()

    load_t.wait()
    thi[...] = t[...].astype(BF16)
    tlo[...] = (t[...] - thi[...].astype(F32)).astype(BF16)

    sent(near_first)
    start(near_rest[:2])
    arrive(near_first[:2])
    start(onward[:2])
    start(near_rest[2:])
    load_a.wait()
    arrive(near_first[2:])

    def reduce_start(source, buf, ss, rs, rows, peers, index):
        out = []
        for o in range(1, peers[0]):
            part = pl.ds(pl.multiple_of(index(o) * rows, rows), rows)
            out.append(remote(source.at[part, :], buf.at[o], ss.at[o], rs.at[o], peers[1](o)))
        return out

    gp = x * ny + y
    gpart = N // (nx * ny)
    mine_g = pl.ds(pl.multiple_of(gp * gpart, gpart), gpart)
    zc = z * 2 + core
    g1 = reduce_start(
        g, gslots, gs1, gr1, gpart, (nx * ny, at_xy), lambda o: along_x(o // ny) * ny + along_y(o % ny)
    )
    g2 = [remote(gz.at[zc], gz.at[zc], gs2.at[o], gr2.at[o], at_zc(o)) for o in range(1, 2 * nz)]
    g3 = [remote(gsum.at[mine_g, :], gsum.at[mine_g, :], gs3.at[o], gr3.at[o], at_xy(o)) for o in range(1, nx * ny)]

    part = at[:, columns(x)]
    g[...] = dot(part, part, ((1,), (1,)), HIGH)
    start(g1)
    arrive(near_rest[:2])
    start(onward[2:])

    half = N // 2
    cpart = half // Q
    cowner = [[x, xp], [xm, x2]]
    mine_c = pl.ds(pl.multiple_of(q * cpart, cpart), cpart)
    c1, c2, c3 = [], [], []
    per = w // cpart
    for h in range(2):
        here = jnp.where(q < per, cowner[h][0], cowner[h][1]) * w + lax.rem(q, per) * cpart
        rows = pl.ds(pl.multiple_of(here, cpart), cpart)
        c1.append(
            reduce_start(
                c.at[h], cslots.at[h], cs1.at[h], cr1.at[h], cpart, (Q, at_q), lambda o: lax.rem(q + o, Q)
            )
        )
        c2.append(
            [remote(cz.at[h, z], cz.at[h, z], cs2.at[h, o], cr2.at[h, o], at_z(o)) for o in range(1, nz)]
        )
        c3.append(
            [remote(csum.at[rows, :], csum.at[rows, :], cs3.at[h, o], cr3.at[h, o], at_q(o)) for o in range(1, Q)]
        )

    def product(h):
        for i, owner in enumerate(cowner[h]):
            hi, lo = split(at[pl.ds(pl.multiple_of(owner * w, w), w), :])
            both = dot(jnp.concatenate([hi, lo], axis=0), thi[...])
            c[h, i * w : (i + 1) * w, :] = both[:w] + both[w:] + dot(hi, tlo[...])

    def sum_scattered(h):
        total = c[h, mine_c, :]
        for o in range(1, Q):
            total = total + cslots[h, o]
        cz[h, z] = total

    def sum_exchanged(h):
        total = cz[h, 0]
        for o in range(1, nz):
            total = total + cz[h, o]
        here = jnp.where(q < per, cowner[h][0], cowner[h][1]) * w + lax.rem(q, per) * cpart
        csum[pl.ds(pl.multiple_of(here, cpart), cpart), :] = total

    @pl.when(root)
    def _():
        lead_a.wait()
        lead_t.wait()

    @pl.when(first & jnp.logical_not(root))
    def _():
        a1_to_q(1).wait_recv()
        t1_to_q(1).wait_recv()

    @pl.when(first)
    def _():
        for o in range(1, nz):
            a1_to_z(o).start()
        for o in range(1, nz):
            t1_to_z(o).start()

    arrive(g1)
    total = g[mine_g, :]
    for o in range(1, nx * ny):
        total = total + gslots[o]
    gz[zc] = total
    start(g2)

    @pl.when(jnp.logical_not(first))
    def _():
        a1_to_z(1).wait_recv()

    start(a1_gather)
    arrive([near_rest[3], near_rest[5]])
    product(0)
    start(c1[0])
    arrive([near_rest[2], near_rest[4]] + onward)
    product(1)
    start(c1[1])

    arrive(g2)
    total = gz[0]
    for o in range(1, 2 * nz):
        total = total + gz[o]
    gsum[mine_g, :] = total
    start(g3)

    @pl.when(jnp.logical_not(first))
    def _():
        t1_to_z(1).wait_recv()

    start(t1_gather)
    for i in range(0, at.shape[1], N):
        hi, lo = split(at[:, i : i + N].T)
        ahi_out[i : i + N, :] = hi
        alo_out[i : i + N, :] = lo
    arrive(a1_gather)
    a1 = a1t[...].T
    row = lax.broadcasted_iota(jnp.int32, (N, N), 0)
    col = lax.broadcasted_iota(jnp.int32, (N, N), 1)
    m2[0:N, :] = a1
    m2[N : 2 * N, :] = jnp.where(row == col, 1.0, 0.0)
    arrive(g3)

    lane = lax.broadcasted_iota(jnp.int32, (8, N), 1)
    sub = lax.broadcasted_iota(jnp.int32, (8, N), 0)
    blocks = N // 8
    m1[...] = gsum[...]
    for b in range(blocks + 1):
        for h in range(2):
            if b == (1, 4)[h]:
                arrive(c1[h])
                sum_scattered(h)
                start(c2[h])
            if b == (9, 13)[h]:
                arrive(c2[h])
                sum_exchanged(h)
                start(c3[h])
        steps, pivots = [], []
        if b < blocks:
            steps.append(eliminate(m1, b, False, pivots))
        if b > 0:
            steps.append(eliminate(m2, b - 1, True, []))
        interleave(*steps)
        if b < blocks:
            rows = slice(8 * b, 8 * b + 8)
            scale = lax.rsqrt(pivots[0])
            diagonal = sub + 8 * b
            block = m1[rows, :] * scale
            upper = jnp.where(lane >= diagonal, block, 0.0)
            inverse = jnp.where(lane < diagonal, block, jnp.where(lane == diagonal, scale, 0.0))
            lead = a1[8 * b : 8 * b + 8, :]
            diag = jnp.sum(lead * inverse, axis=1, keepdims=True)
            sign = jnp.where(diag >= 0, -1.0, 1.0)
            signed = sign * upper
            r_out[rows, :] = signed
            rit[rows, :] = sign * inverse
            bmat[rows, :] = lead - signed
            m2[rows, :] = m2[rows, :] - signed
    v = jnp.where(row <= col, m2[N : 2 * N, :], 0.0)
    linv = jnp.where(row == col, 1.0, jnp.where(row > col, m2[0:N, :], 0.0))
    vt = v.T
    m1[...] = vt
    vxt_out[...] = m1[own, :]
    l1t = jnp.where(row == col, 1.0, jnp.where(row < col, dot(vt, bmat[...], ((1,), (1,)), HIGH), 0.0))
    m1[...] = l1t
    l1xt_out[...] = m1[own, :]
    arrive(c3[0] + c3[1] + t1_gather)
    d = dot(rit[...], csum[...], precision=HIGH)
    d_out[...] = d
    k_out[...] = dot(v, dot(linv, t1[...] - d, precision=HIGH), precision=HIGH)

    sent(near_rest + onward + g1 + g2 + g3)
    for h in range(2):
        sent(c1[h] + c2[h] + c3[h])
    sent(t1_gather + a1_gather)

    @pl.when(root)
    def _():
        sent([t1_to_q(o) for o in range(1, Q)])
        sent([a1_to_q(o) for o in range(1, Q)])

    @pl.when(first)
    def _():
        sent([t1_to_z(o) for o in range(1, nz)])
        sent([a1_to_z(o) for o in range(1, nz)])


def update_kernel(t_ref, ahi_ref, alo_ref, k_ref, d_ref, vxt_ref, l1xt_ref, r_ref, out_ref, yt_ref, factor_ref):
    ahi, alo = ahi_ref[...], alo_ref[...]
    khi, klo = split(k_ref[...])
    a2 = jnp.concatenate([ahi, alo], axis=1)
    k2 = jnp.concatenate([khi, khi], axis=0)
    out_ref[...] = t_ref[...] - (dot(a2, k2) + dot(ahi, klo))
    vhi, vlo = split(vxt_ref[...])
    nt = ((1,), (1,))
    yt_ref[...] = dot(vhi, ahi, nt) + dot(vhi, alo, nt) + dot(vlo, ahi, nt)

    factor_ref[...] = r_ref[...]

    @pl.when((lax.axis_index("row") == 0) & (pl.program_id(0) == 0))
    def _():
        out_ref[0:N, :] = d_ref[...]
        yt_ref[:, 0:N] = l1xt_ref[...]


def per_device(nz, nx, panel_block, trailing):
    rows, cols = trailing.shape
    w = N // nx
    dma = pltpu.SemaphoreType.DMA
    any_spec = pl.BlockSpec(memory_space=pltpu.HBM)
    vmem = pl.BlockSpec(memory_space=pltpu.VMEM)
    hbm = functools.partial(pltpu.with_memory_space_constraint, memory_space=pltpu.HBM)
    shape = jax.ShapeDtypeStruct
    ahi, alo, k, d, vxt, l1xt, factor = pl.pallas_call(
        functools.partial(factor_kernel, nz, nx),
        out_shape=[
            shape((rows, N), BF16), shape((rows, N), BF16), shape((N, cols), F32), shape((N, cols), F32),
            shape((w, N), F32), shape((w, N), F32), shape((N, N), F32),
        ],
        in_specs=[any_spec, any_spec],
        out_specs=[vmem] * 7,
        scratch_shapes=[
            pltpu.VMEM((N, rows), F32), pltpu.VMEM((rows, cols), F32), pltpu.VMEM((rows, cols), BF16),
            pltpu.VMEM((rows, cols), BF16), pltpu.VMEM((N, N), F32), pltpu.VMEM((N, cols), F32),
            pltpu.VMEM((N, N), F32), pltpu.VMEM((16, 8, N), F32), pltpu.VMEM((2 * nz, 8, N), F32), pltpu.VMEM((N, N), F32),
            pltpu.VMEM((2, N // 2, cols), F32), pltpu.VMEM((2, Q, N // 16, cols), F32),
            pltpu.VMEM((2, nz, N // 16, cols), F32), pltpu.VMEM((N, cols), F32),
            pltpu.VMEM((N, N), F32), pltpu.VMEM((2 * N, N), F32), pltpu.VMEM((N, N), F32), pltpu.VMEM((N, N), F32),
            dma((4,)), dma((13,)), dma((13,)),
        ] + [dma((16,))] * 6 + [dma((2, 8))] * 6 + [
            dma((8,)), dma((1,)), dma((8,)), dma((1,)), dma((8,)), dma((8,)),
            dma((8,)), dma((1,)), dma((8,)), dma((1,)), dma((nx,)), dma((nx,)),
        ],
        compiler_params=pltpu.CompilerParams(
            collective_id=0, has_side_effects=True, vmem_limit_bytes=48 * 1024 * 1024
        ),
        name="factor",
    )(hbm(panel_block.T), hbm(trailing))
    tile = 512
    updated, yt, factor = pl.pallas_call(
        update_kernel,
        grid=(rows // tile,),
        out_shape=[shape((rows, cols), F32), shape((w, rows), F32), shape((N, N), F32)],
        in_specs=[
            pl.BlockSpec((tile, cols), lambda i: (i, 0)), pl.BlockSpec((tile, N), lambda i: (i, 0)),
            pl.BlockSpec((tile, N), lambda i: (i, 0)), pl.BlockSpec((N, cols), lambda i: (0, 0)),
            pl.BlockSpec((N, cols), lambda i: (0, 0)), pl.BlockSpec((w, N), lambda i: (0, 0)),
            pl.BlockSpec((w, N), lambda i: (0, 0)), pl.BlockSpec((N, N), lambda i: (0, 0)),
        ],
        out_specs=[
            pl.BlockSpec((tile, cols), lambda i: (i, 0)), pl.BlockSpec((w, tile), lambda i: (0, i)),
            pl.BlockSpec((N, N), lambda i: (0, 0)),
        ],
        compiler_params=pltpu.CompilerParams(vmem_limit_bytes=32 * 1024 * 1024),
        name="update",
    )(trailing, ahi, alo, k, d, vxt, l1xt, factor)
    return updated, yt.T, factor


def solution(mesh):
    nz, nx = mesh.shape["row"] // Q, mesh.shape["col"]
    in_specs = (P("row", "col"), P("row", "col"))
    out_specs = (P("row", "col"), P("row", "col"), P())
    return jax.shard_map(
        functools.partial(per_device, nz, nx), mesh=mesh, in_specs=in_specs, out_specs=out_specs, check_vma=False
    )
```

```python
import functools

import jax
import jax.numpy as jnp
from jax import lax
from jax.experimental import pallas as pl
from jax.experimental.pallas import tpu as pltpu
from jax.sharding import PartitionSpec as P

F32 = jnp.float32
BF16 = jnp.bfloat16
HIGH = lax.Precision.HIGHEST
N = 128
Q = 8


def dot(a, b, dims=((1,), (0,)), precision=None):
    return lax.dot_general(a, b, (dims, ((), ())), precision=precision, preferred_element_type=F32)


def split(x):
    hi = x.astype(BF16)
    return hi, (x - hi.astype(F32)).astype(BF16)


def dot3(a, b):
    (ah, al), (bh, bl) = split(a), split(b)
    return dot(ah, bh) + (dot(ah, bl) + dot(al, bh))


def eliminate(m_ref, b, bottom, out):
    r0 = 8 * b
    lane = lax.broadcasted_iota(jnp.int32, (8, N), 1)
    sub = lax.broadcasted_iota(jnp.int32, (8, N), 0)
    parts = []
    if r0 + 8 < N:
        parts.append((r0 + 8, N - r0 - 8, False))
    if bottom:
        parts.append((N, r0 + 8, True))
    rows = m_ref[r0 : r0 + 8, :]
    rest = [m_ref[s : s + n, :] for s, n, _ in parts]
    cols = [
        [jnp.broadcast_to(p[:, r0 + j : r0 + j + 1], (p.shape[0], N)) for j in range(8)]
        for p in [rows] + rest
    ]
    mults, pivots = [], None
    for k in range(8):
        yield
        c0 = cols[0][k]
        d = jnp.broadcast_to(c0[k : k + 1, :], (8, N))
        inv = 1.0 / d
        pivots = d if pivots is None else jnp.where(sub == k, d, pivots)
        ms = [jnp.where(sub > k, c0 * inv, 0.0)] + [c[k] * inv[0:1, :] for c in cols[1:]]
        mults.append(ms)
        for j in range(k + 1, 8):
            top = cols[0][j][k : k + 1, :]
            for i in range(len(cols)):
                cols[i][j] = cols[i][j] - ms[i] * top
    pivot_rows = []
    for k in range(8):
        lk = r0 + k
        row = jnp.where(lane[0:1] == lk, 1.0, rows[k : k + 1, :])
        rows = jnp.where((lane == lk) & (sub > k), 0.0, rows) - mults[k][0] * row
        pivot_rows.append(jnp.where((lane[0:1] > lk) & (lane[0:1] < r0 + 8), 0.0, row))
    for i, (s, n, low) in enumerate(parts):
        lane_n = lax.broadcasted_iota(jnp.int32, (n, N), 1)
        acc = jnp.where((lane_n >= r0) & (lane_n < r0 + 8), 0.0, rest[i])
        for k in range(8):
            row = jnp.where(lane[0:1] >= r0 + 8, pivot_rows[k], 0.0) if low else pivot_rows[k]
            acc = acc - mults[k][i + 1] * row
        if low:
            for k in range(8):
                acc = jnp.where(lane_n == r0 + k, mults[k][i + 1], acc)
        m_ref[s : s + n, :] = acc
    m_ref[r0 : r0 + 8, :] = rows
    out.append(pivots)


def interleave(*steps):
    steps = list(steps)
    while steps:
        for step in list(steps):
            if next(step, True) is True:
                steps.remove(step)


def remote(src, dst, send, recv, device):
    return pltpu.make_async_remote_copy(
        src_ref=src, dst_ref=dst, send_sem=send, recv_sem=recv, device_id=device, device_id_type=pl.DeviceIdType.MESH
    )


def factor_kernel(
    nz, nx,
    pt_ref, t_ref,
    ahi_out, alo_out, k_out, d_out, vxt_out, l1xt_out, r_out,
    at, t, thi, tlo, a1t, t1, g, gslots, gz, gsum, c, cslots, cz, csum, m1, m2, rit, bmat, t1x,
    load_sem, xs, xr, gs1, gr1, gs2, gr2, gs3, gr3, cs1, cr1, cs2, cr2, cs3, cr3, ts1, tr1, ts2, tr2, ts3, tr3,
    as1, ar1, as2, ar2, as3, ar3,
):
    r = lax.axis_index("row")
    x = lax.axis_index("col")
    z, q = lax.div(r, Q), lax.rem(r, Q)
    ny = Q // 2
    y, core = lax.div(q, 2), lax.rem(q, 2)
    w = N // nx
    seg = pt_ref.shape[1] // nx

    def along_x(o):
        return lax.rem(x + o, nx)

    def along_y(o):
        return lax.rem(y + o, ny)

    def at_x(o):
        return {"col": along_x(o)}

    def at_q(o):
        return {"row": z * Q + lax.rem(q + o, Q)}

    def at_z(o):
        return {"row": lax.rem(z + o, nz) * Q + q}

    def at_xy(o):
        return {"row": z * Q + along_y(o % ny) * 2 + core, "col": along_x(o // ny)}

    def at_zc(o):
        return {"row": lax.rem(z + o // 2, nz) * Q + y * 2 + lax.rem(core + o % 2, 2)}

    load_t = pltpu.make_async_copy(t_ref, t, load_sem.at[0])
    load_t.start()
    own = pl.ds(pl.multiple_of(x * w, w), w)
    load_a = pltpu.make_async_copy(pt_ref, at.at[own, :], load_sem.at[1])
    load_a.start()

    barrier = pltpu.get_barrier_semaphore()
    greeted = [at_xy(o) for o in range(1, nx * ny)] + [at_zc(o) for o in range(1, 2 * nz)]
    greeted += [{"row": z * Q + along_y(o) * 2 + (1 - core)} for o in range(1, ny)]
    for device in greeted:
        pl.semaphore_signal(barrier, inc=1, device_id=device, device_id_type=pl.DeviceIdType.MESH)
    pl.semaphore_wait(barrier, len(greeted))

    def columns(s):
        return pl.ds(pl.multiple_of(s * seg, seg), seg)

    def strip(owner, cols):
        return at.at[pl.ds(pl.multiple_of(owner * w, w), w), cols]

    def tell(i, o, s):
        return remote(pt_ref.at[:, columns(s)], strip(x, columns(s)), xs.at[i], xr.at[i], at_x(o))

    def forward(i, o, owner, cols):
        return remote(strip(owner, cols), strip(owner, cols), xs.at[i], xr.at[i], at_x(o))

    xp, xm, x2 = along_x(1), along_x(nx - 1), along_x(2)
    plus, minus = 1, nx - 1
    first_half = pl.ds(pl.multiple_of(xm * seg, seg), seg // 2)
    second_half = pl.ds(pl.multiple_of(xp * seg + seg // 2, seg // 2), seg // 2)
    near_first = [tell(0, plus, xp), tell(1, minus, xm), tell(2, 2, x2)]
    near_rest = [
        tell(3, plus, x), tell(4, minus, x), tell(5, plus, x2), tell(6, minus, x2), tell(7, plus, xm), tell(8, minus, xp),
    ]
    onward = [
        forward(9, plus, xm, columns(x)), forward(10, minus, xp, columns(x)),
        forward(11, plus, xm, first_half), forward(12, minus, xp, second_half),
    ]

    def start(copies):
        for copy in copies:
            copy.start()

    def arrive(copies):
        for copy in copies:
            copy.wait_recv()

    def sent(copies):
        for copy in copies:
            copy.wait_send()

    start(near_first)

    root = r == 0
    first = z == 0
    piece = N // Q
    mine_piece = pl.ds(pl.multiple_of(q * piece, piece), piece)
    lead_cols = pl.ds(0, N)

    def t1_to_q(o):
        rows = pl.ds(pl.multiple_of(lax.rem(q + o, Q) * piece, piece), piece)
        return remote(t_ref.at[rows, :], t1.at[rows, :], ts1.at[o], tr1.at[0], at_q(o))

    def a1_to_q(o):
        return remote(pt_ref.at[:, lead_cols], a1t.at[own, :], as1.at[o], ar1.at[0], at_q(o))

    def t1_to_z(o):
        return remote(t1.at[mine_piece, :], t1.at[mine_piece, :], ts2.at[o], tr2.at[0], at_z(o))

    def a1_to_z(o):
        return remote(a1t.at[own, :], a1t.at[own, :], as2.at[o], ar2.at[0], at_z(o))

    t1_gather = [
        remote(t1.at[mine_piece, :], t1.at[mine_piece, :], ts3.at[o], tr3.at[o], at_q(o)) for o in range(1, Q)
    ]
    a1_gather = [remote(a1t.at[own, :], a1t.at[own, :], as3.at[o], ar3.at[o], at_x(o)) for o in range(1, nx)]
    lead_t = pltpu.make_async_copy(t_ref.at[mine_piece, :], t1.at[mine_piece, :], load_sem.at[2])
    lead_a = pltpu.make_async_copy(pt_ref.at[:, lead_cols], a1t.at[own, :], load_sem.at[3])

    @pl.when(root)
    def _():
        for o in range(1, Q):
            a1_to_q(o).start()
        lead_a.start()
        lead_t.start()
        for o in range(1, Q):
            t1_to_q(o).start()

    load_t.wait()
    thi[...] = t[...].astype(BF16)
    tlo[...] = (t[...] - thi[...].astype(F32)).astype(BF16)

    sent(near_first)
    start(near_rest[:2])
    arrive(near_first[:2])
    start(onward[:2])
    start(near_rest[2:])
    load_a.wait()
    arrive(near_first[2:])

    def reduce_start(source, buf, ss, rs, rows, peers, index):
        out = []
        for o in range(1, peers[0]):
            part = pl.ds(pl.multiple_of(index(o) * rows, rows), rows)
            out.append(remote(source.at[part, :], buf.at[o], ss.at[o], rs.at[o], peers[1](o)))
        return out

    gp = x * ny + y
    gpart = N // (nx * ny)
    mine_g = pl.ds(pl.multiple_of(gp * gpart, gpart), gpart)
    zc = z * 2 + core
    g1 = reduce_start(
        g, gslots, gs1, gr1, gpart, (nx * ny, at_xy), lambda o: along_x(o // ny) * ny + along_y(o % ny)
    )
    g2 = [remote(gz.at[zc], gz.at[zc], gs2.at[o], gr2.at[o], at_zc(o)) for o in range(1, 2 * nz)]
    g3 = [remote(gsum.at[mine_g, :], gsum.at[mine_g, :], gs3.at[o], gr3.at[o], at_xy(o)) for o in range(1, nx * ny)]

    part = at[:, columns(x)]
    g[...] = dot(part, part, ((1,), (1,)), HIGH)
    start(g1)
    arrive(near_rest[:2])
    start(onward[2:])

    half = N // 2
    cpart = half // Q
    cowner = [[x, xp], [xm, x2]]
    mine_c = pl.ds(pl.multiple_of(q * cpart, cpart), cpart)
    c1, c2, c3 = [], [], []
    per = w // cpart
    for h in range(2):
        here = jnp.where(q < per, cowner[h][0], cowner[h][1]) * w + lax.rem(q, per) * cpart
        rows = pl.ds(pl.multiple_of(here, cpart), cpart)
        c1.append(
            reduce_start(
                c.at[h], cslots.at[h], cs1.at[h], cr1.at[h], cpart, (Q, at_q), lambda o: lax.rem(q + o, Q)
            )
        )
        c2.append(
            [remote(cz.at[h, z], cz.at[h, z], cs2.at[h, o], cr2.at[h, o], at_z(o)) for o in range(1, nz)]
        )
        c3.append(
            [remote(csum.at[rows, :], csum.at[rows, :], cs3.at[h, o], cr3.at[h, o], at_q(o)) for o in range(1, Q)]
        )

    def product(h):
        for i, owner in enumerate(cowner[h]):
            hi, lo = split(at[pl.ds(pl.multiple_of(owner * w, w), w), :])
            both = dot(jnp.concatenate([hi, lo], axis=0), thi[...])
            c[h, i * w : (i + 1) * w, :] = both[:w] + both[w:] + dot(hi, tlo[...])

    def sum_scattered(h):
        total = c[h, mine_c, :]
        for o in range(1, Q):
            total = total + cslots[h, o]
        cz[h, z] = total

    def sum_exchanged(h):
        total = cz[h, 0]
        for o in range(1, nz):
            total = total + cz[h, o]
        here = jnp.where(q < per, cowner[h][0], cowner[h][1]) * w + lax.rem(q, per) * cpart
        csum[pl.ds(pl.multiple_of(here, cpart), cpart), :] = total

    @pl.when(root)
    def _():
        lead_a.wait()

    @pl.when(first & jnp.logical_not(root))
    def _():
        a1_to_q(1).wait_recv()

    @pl.when(first)
    def _():
        for o in range(1, nz):
            a1_to_z(o).start()

    arrive(g1)
    total = g[mine_g, :]
    for o in range(1, nx * ny):
        total = total + gslots[o]
    gz[zc] = total
    start(g2)

    @pl.when(jnp.logical_not(first))
    def _():
        a1_to_z(1).wait_recv()

    start(a1_gather)
    arrive([near_rest[3], near_rest[5]])
    product(0)
    start(c1[0])
    arrive([near_rest[2], near_rest[4]] + onward)
    product(1)
    start(c1[1])

    @pl.when(root)
    def _():
        lead_t.wait()

    @pl.when(first & jnp.logical_not(root))
    def _():
        t1_to_q(1).wait_recv()

    @pl.when(first)
    def _():
        for o in range(1, nz):
            t1_to_z(o).start()

    arrive(g2)
    total = gz[0]
    for o in range(1, 2 * nz):
        total = total + gz[o]
    gsum[mine_g, :] = total
    start(g3)
    arrive(c1[0])
    sum_scattered(0)
    start(c2[0])
    for i in range(0, at.shape[1], N):
        hi, lo = split(at[:, i : i + N].T)
        ahi_out[i : i + N, :] = hi
        alo_out[i : i + N, :] = lo
    arrive(c1[1])
    sum_scattered(1)
    start(c2[1])
    arrive(a1_gather)
    a1 = a1t[...].T
    row = lax.broadcasted_iota(jnp.int32, (N, N), 0)
    col = lax.broadcasted_iota(jnp.int32, (N, N), 1)
    m2[0:N, :] = a1
    m2[N : 2 * N, :] = jnp.where(row == col, 1.0, 0.0)
    arrive(g3)

    lane = lax.broadcasted_iota(jnp.int32, (8, N), 1)
    sub = lax.broadcasted_iota(jnp.int32, (8, N), 0)
    blocks = N // 8
    m1[...] = gsum[...]
    for b in range(blocks + 1):
        for h in range(2):
            if b == (2, 5)[h]:
                arrive(c2[h])
                sum_exchanged(h)
                start(c3[h])
        if b == 7:

            @pl.when(jnp.logical_not(first))
            def _():
                t1_to_z(1).wait_recv()

            start(t1_gather)
        if b == blocks:
            arrive(c3[0] + c3[1] + t1_gather)
            d = dot3(rit[...], csum[...])
            d_out[...] = d
            t1x[...] = t1[...] - d
        steps, pivots = [], []
        if b < blocks:
            steps.append(eliminate(m1, b, False, pivots))
        if b > 0:
            steps.append(eliminate(m2, b - 1, True, []))
        interleave(*steps)
        if b < blocks:
            rows = slice(8 * b, 8 * b + 8)
            scale = lax.rsqrt(pivots[0])
            diagonal = sub + 8 * b
            block = m1[rows, :] * scale
            upper = jnp.where(lane >= diagonal, block, 0.0)
            inverse = jnp.where(lane < diagonal, block, jnp.where(lane == diagonal, scale, 0.0))
            lead = a1[8 * b : 8 * b + 8, :]
            diag = jnp.sum(lead * inverse, axis=1, keepdims=True)
            sign = jnp.where(diag >= 0, -1.0, 1.0)
            signed = sign * upper
            r_out[rows, :] = signed
            rit[rows, :] = sign * inverse
            bmat[rows, :] = lead - signed
            m2[rows, :] = m2[rows, :] - signed
    v = jnp.where(row <= col, m2[N : 2 * N, :], 0.0)
    linv = jnp.where(row == col, 1.0, jnp.where(row > col, m2[0:N, :], 0.0))
    k_out[...] = dot3(v, dot3(linv, t1x[...]))
    vt = v.T
    m1[...] = vt
    vxt_out[...] = m1[own, :]
    l1t = jnp.where(row == col, 1.0, jnp.where(row < col, dot(vt, bmat[...], ((1,), (1,)), HIGH), 0.0))
    m1[...] = l1t
    l1xt_out[...] = m1[own, :]
    sent(near_rest + onward + g1 + g2 + g3)
    for h in range(2):
        sent(c1[h] + c2[h] + c3[h])
    sent(t1_gather + a1_gather)

    @pl.when(root)
    def _():
        sent([t1_to_q(o) for o in range(1, Q)])
        sent([a1_to_q(o) for o in range(1, Q)])

    @pl.when(first)
    def _():
        sent([t1_to_z(o) for o in range(1, nz)])
        sent([a1_to_z(o) for o in range(1, nz)])


def update_kernel(t_ref, ahi_ref, alo_ref, k_ref, d_ref, vxt_ref, l1xt_ref, r_ref, out_ref, yt_ref, factor_ref):
    ahi, alo = ahi_ref[...], alo_ref[...]
    khi, klo = split(k_ref[...])
    a2 = jnp.concatenate([ahi, alo], axis=1)
    k2 = jnp.concatenate([khi, khi], axis=0)
    out_ref[...] = t_ref[...] - (dot(a2, k2) + dot(ahi, klo))
    vhi, vlo = split(vxt_ref[...])
    nt = ((1,), (1,))
    yt_ref[...] = dot(vhi, ahi, nt) + dot(vhi, alo, nt) + dot(vlo, ahi, nt)

    factor_ref[...] = r_ref[...]

    @pl.when((lax.axis_index("row") == 0) & (pl.program_id(0) == 0))
    def _():
        out_ref[0:N, :] = d_ref[...]
        yt_ref[:, 0:N] = l1xt_ref[...]


def per_device(nz, nx, panel_block, trailing):
    rows, cols = trailing.shape
    w = N // nx
    dma = pltpu.SemaphoreType.DMA
    any_spec = pl.BlockSpec(memory_space=pltpu.HBM)
    vmem = pl.BlockSpec(memory_space=pltpu.VMEM)
    hbm = functools.partial(pltpu.with_memory_space_constraint, memory_space=pltpu.HBM)
    shape = jax.ShapeDtypeStruct
    ahi, alo, k, d, vxt, l1xt, factor = pl.pallas_call(
        functools.partial(factor_kernel, nz, nx),
        out_shape=[
            shape((rows, N), BF16), shape((rows, N), BF16), shape((N, cols), F32), shape((N, cols), F32),
            shape((w, N), F32), shape((w, N), F32), shape((N, N), F32),
        ],
        in_specs=[any_spec, any_spec],
        out_specs=[vmem] * 7,
        scratch_shapes=[
            pltpu.VMEM((N, rows), F32), pltpu.VMEM((rows, cols), F32), pltpu.VMEM((rows, cols), BF16),
            pltpu.VMEM((rows, cols), BF16), pltpu.VMEM((N, N), F32), pltpu.VMEM((N, cols), F32),
            pltpu.VMEM((N, N), F32), pltpu.VMEM((16, 8, N), F32), pltpu.VMEM((2 * nz, 8, N), F32), pltpu.VMEM((N, N), F32),
            pltpu.VMEM((2, N // 2, cols), F32), pltpu.VMEM((2, Q, N // 16, cols), F32),
            pltpu.VMEM((2, nz, N // 16, cols), F32), pltpu.VMEM((N, cols), F32),
            pltpu.VMEM((N, N), F32), pltpu.VMEM((2 * N, N), F32), pltpu.VMEM((N, N), F32), pltpu.VMEM((N, N), F32),
            pltpu.VMEM((N, cols), F32),
            dma((4,)), dma((13,)), dma((13,)),
        ] + [dma((16,))] * 6 + [dma((2, 8))] * 6 + [
            dma((8,)), dma((1,)), dma((8,)), dma((1,)), dma((8,)), dma((8,)),
            dma((8,)), dma((1,)), dma((8,)), dma((1,)), dma((nx,)), dma((nx,)),
        ],
        compiler_params=pltpu.CompilerParams(
            collective_id=0, has_side_effects=True, vmem_limit_bytes=48 * 1024 * 1024
        ),
        name="factor",
    )(hbm(panel_block.T), hbm(trailing))
    tile = 256
    updated, yt, factor = pl.pallas_call(
        update_kernel,
        grid=(rows // tile,),
        out_shape=[shape((rows, cols), F32), shape((w, rows), F32), shape((N, N), F32)],
        in_specs=[
            pl.BlockSpec((tile, cols), lambda i: (i, 0)), pl.BlockSpec((tile, N), lambda i: (i, 0)),
            pl.BlockSpec((tile, N), lambda i: (i, 0)), pl.BlockSpec((N, cols), lambda i: (0, 0)),
            pl.BlockSpec((N, cols), lambda i: (0, 0)), pl.BlockSpec((w, N), lambda i: (0, 0)),
            pl.BlockSpec((w, N), lambda i: (0, 0)), pl.BlockSpec((N, N), lambda i: (0, 0)),
        ],
        out_specs=[
            pl.BlockSpec((tile, cols), lambda i: (i, 0)), pl.BlockSpec((w, tile), lambda i: (0, i)),
            pl.BlockSpec((N, N), lambda i: (0, 0)),
        ],
        compiler_params=pltpu.CompilerParams(vmem_limit_bytes=32 * 1024 * 1024),
        name="update",
    )(trailing, ahi, alo, k, d, vxt, l1xt, factor)
    return updated, yt.T, factor


def solution(mesh):
    nz, nx = mesh.shape["row"] // Q, mesh.shape["col"]
    in_specs = (P("row", "col"), P("row", "col"))
    out_specs = (P("row", "col"), P("row", "col"), P())
    return jax.shard_map(
        functools.partial(per_device, nz, nx), mesh=mesh, in_specs=in_specs, out_specs=out_specs, check_vma=False
    )
```

```python
import functools

import jax
import jax.numpy as jnp
from jax import lax
from jax.experimental import pallas as pl
from jax.experimental.pallas import tpu as pltpu
from jax.sharding import PartitionSpec as P

F32 = jnp.float32
BF16 = jnp.bfloat16
HIGH = lax.Precision.HIGHEST
N = 128
Q = 8


def dot(a, b, dims=((1,), (0,)), precision=None):
    return lax.dot_general(a, b, (dims, ((), ())), precision=precision, preferred_element_type=F32)


def split(x):
    hi = x.astype(BF16)
    return hi, (x - hi.astype(F32)).astype(BF16)


def dot3(a, b):
    (ah, al), (bh, bl) = split(a), split(b)
    return dot(ah, bh) + (dot(ah, bl) + dot(al, bh))


def eliminate(m_ref, b, bottom, out):
    r0 = 8 * b
    lane = lax.broadcasted_iota(jnp.int32, (8, N), 1)
    sub = lax.broadcasted_iota(jnp.int32, (8, N), 0)
    parts = []
    if r0 + 8 < N:
        parts.append((r0 + 8, N - r0 - 8, False))
    if bottom:
        parts.append((N, r0 + 8, True))
    rows = m_ref[r0 : r0 + 8, :]
    rest = [m_ref[s : s + n, :] for s, n, _ in parts]
    cols = [
        [jnp.broadcast_to(p[:, r0 + j : r0 + j + 1], (p.shape[0], N)) for j in range(8)]
        for p in [rows] + rest
    ]
    mults, pivots = [], None
    for k in range(8):
        yield
        c0 = cols[0][k]
        d = jnp.broadcast_to(c0[k : k + 1, :], (8, N))
        inv = 1.0 / d
        pivots = d if pivots is None else jnp.where(sub == k, d, pivots)
        ms = [jnp.where(sub > k, c0 * inv, 0.0)] + [c[k] * inv[0:1, :] for c in cols[1:]]
        mults.append(ms)
        for j in range(k + 1, 8):
            top = cols[0][j][k : k + 1, :]
            for i in range(len(cols)):
                cols[i][j] = cols[i][j] - ms[i] * top
    pivot_rows = []
    for k in range(8):
        lk = r0 + k
        row = jnp.where(lane[0:1] == lk, 1.0, rows[k : k + 1, :])
        rows = jnp.where((lane == lk) & (sub > k), 0.0, rows) - mults[k][0] * row
        pivot_rows.append(jnp.where((lane[0:1] > lk) & (lane[0:1] < r0 + 8), 0.0, row))
    for i, (s, n, low) in enumerate(parts):
        lane_n = lax.broadcasted_iota(jnp.int32, (n, N), 1)
        acc = jnp.where((lane_n >= r0) & (lane_n < r0 + 8), 0.0, rest[i])
        for k in range(8):
            row = jnp.where(lane[0:1] >= r0 + 8, pivot_rows[k], 0.0) if low else pivot_rows[k]
            acc = acc - mults[k][i + 1] * row
        if low:
            for k in range(8):
                acc = jnp.where(lane_n == r0 + k, mults[k][i + 1], acc)
        m_ref[s : s + n, :] = acc
    m_ref[r0 : r0 + 8, :] = rows
    out.append(pivots)


def interleave(*steps):
    steps = list(steps)
    while steps:
        for step in list(steps):
            if next(step, True) is True:
                steps.remove(step)


def remote(src, dst, send, recv, device):
    return pltpu.make_async_remote_copy(
        src_ref=src, dst_ref=dst, send_sem=send, recv_sem=recv, device_id=device, device_id_type=pl.DeviceIdType.MESH
    )


def factor_kernel(
    nz, nx,
    pt_ref, t_ref,
    ahi_out, alo_out, khi_out, klo_out, d_out, vxt_out, l1xt_out, r_out,
    at, t, thi, tlo, a1t, t1, g, gslots, gz, gsum, strips, csum, m1, m2, rit, bmat, t1x, p0, p1, p2, s0, s1, s2, z0, z1, z2, e0, e1, e2,
    load_sem, xs, xr, gs1, gr1, gs2, gr2, gs3, gr3, cs1, cr1, cs2, cr2, cs3, cr3, ts1, tr1, ts2, tr2, ts3, tr3,
    as1, ar1, as2, ar2, as3, ar3,
):
    cparts, cslots, cz, call = (p0, p1, p2), (s0, s1, s2), (z0, z1, z2), (e0, e1, e2)
    r = lax.axis_index("row")
    x = lax.axis_index("col")
    z, q = lax.div(r, Q), lax.rem(r, Q)
    ny = Q // 2
    y, core = lax.div(q, 2), lax.rem(q, 2)
    w = N // nx
    seg = pt_ref.shape[1] // nx

    def along_x(o):
        return lax.rem(x + o, nx)

    def along_y(o):
        return lax.rem(y + o, ny)

    def at_x(o):
        return {"col": along_x(o)}

    def at_q(o):
        return {"row": z * Q + lax.rem(q + o, Q)}

    def at_z(o):
        return {"row": lax.rem(z + o, nz) * Q + q}

    def at_xy(o):
        return {"row": z * Q + along_y(o % ny) * 2 + core, "col": along_x(o // ny)}

    def at_zc(o):
        return {"row": lax.rem(z + o // 2, nz) * Q + y * 2 + lax.rem(core + o % 2, 2)}

    load_t = pltpu.make_async_copy(t_ref, t, load_sem.at[0])
    load_t.start()
    own = pl.ds(pl.multiple_of(x * w, w), w)
    load_a = pltpu.make_async_copy(pt_ref, at.at[own, :], load_sem.at[1])
    load_a.start()

    barrier = pltpu.get_barrier_semaphore()
    greeted = [at_xy(o) for o in range(1, nx * ny)] + [at_zc(o) for o in range(1, 2 * nz)]
    greeted += [{"row": z * Q + along_y(o) * 2 + (1 - core)} for o in range(1, ny)]
    for device in greeted:
        pl.semaphore_signal(barrier, inc=1, device_id=device, device_id_type=pl.DeviceIdType.MESH)
    pl.semaphore_wait(barrier, len(greeted))

    def columns(s):
        return pl.ds(pl.multiple_of(s * seg, seg), seg)

    def strip(owner, cols):
        return at.at[pl.ds(pl.multiple_of(owner * w, w), w), cols]

    def tell(i, o, s):
        return remote(pt_ref.at[:, columns(s)], strip(x, columns(s)), xs.at[i], xr.at[i], at_x(o))

    def forward(i, o, owner, cols):
        return remote(strip(owner, cols), strip(owner, cols), xs.at[i], xr.at[i], at_x(o))

    xp, xm, x2 = along_x(1), along_x(nx - 1), along_x(2)
    plus, minus = 1, nx - 1
    first_half = pl.ds(pl.multiple_of(xm * seg, seg), seg // 2)
    second_half = pl.ds(pl.multiple_of(xp * seg + seg // 2, seg // 2), seg // 2)
    near_first = [tell(0, plus, xp), tell(1, minus, xm), tell(2, 2, x2)]
    near_rest = [
        tell(3, plus, x), tell(4, minus, x), tell(5, plus, x2), tell(6, minus, x2), tell(7, plus, xm), tell(8, minus, xp),
    ]
    onward = [
        forward(9, plus, xm, columns(x)), forward(10, minus, xp, columns(x)),
        forward(11, plus, xm, first_half), forward(12, minus, xp, second_half),
    ]

    def start(copies):
        for copy in copies:
            copy.start()

    def arrive(copies):
        for copy in copies:
            copy.wait_recv()

    def sent(copies):
        for copy in copies:
            copy.wait_send()

    start(near_first)

    owners = [[x], [xp, xm], [x2]]
    c1, c2, c3 = [], [], []
    for h in range(3):
        c1.append([
            remote(cparts[h].at[lax.rem(q + o, Q)], cslots[h].at[o], cs1.at[h, o], cr1.at[h, o], at_q(o))
            for o in range(1, Q)
        ])
        c2.append([remote(cz[h].at[z], cz[h].at[z], cs2.at[h, o], cr2.at[h, o], at_z(o)) for o in range(1, nz)])
        c3.append([remote(call[h].at[q], call[h].at[q], cs3.at[h, o], cr3.at[h, o], at_q(o)) for o in range(1, Q)])

    def product(h):
        n = len(owners[h]) * w // Q
        for i, owner in enumerate(owners[h]):
            hi, lo = split(at[pl.ds(pl.multiple_of(owner * w, w), w), :])
            both = dot(jnp.concatenate([hi, lo], axis=0), thi[...])
            value = both[:w] + both[w:] + dot(hi, tlo[...])
            for j in range(w // n):
                cparts[h][i * (w // n) + j] = value[j * n : (j + 1) * n, :]
        start(c1[h])

    def sum_scattered(h):
        arrive(c1[h])
        total = cparts[h][q]
        for o in range(1, Q):
            total = total + cslots[h][o]
        cz[h][z] = total
        start(c2[h])

    def sum_exchanged(h):
        arrive(c2[h])
        total = cz[h][0]
        for o in range(1, nz):
            total = total + cz[h][o]
        call[h][q] = total
        start(c3[h])

    def collect():
        for h in range(3):
            n = len(owners[h]) * w // Q
            for i, owner in enumerate(owners[h]):
                for j in range(w // n):
                    strips[i * w + j * n : i * w + (j + 1) * n, :] = call[h][i * (w // n) + j]
                csum[pl.ds(pl.multiple_of(owner * w, w), w), :] = strips[i * w : (i + 1) * w, :]

    root = r == 0
    first = z == 0
    piece = N // Q
    mine_piece = pl.ds(pl.multiple_of(q * piece, piece), piece)
    lead_cols = pl.ds(0, N)

    def t1_to_q(o):
        rows = pl.ds(pl.multiple_of(lax.rem(q + o, Q) * piece, piece), piece)
        return remote(t_ref.at[rows, :], t1.at[rows, :], ts1.at[o], tr1.at[0], at_q(o))

    def a1_to_q(o):
        return remote(pt_ref.at[:, lead_cols], a1t.at[own, :], as1.at[o], ar1.at[0], at_q(o))

    def t1_to_z(o):
        return remote(t1.at[mine_piece, :], t1.at[mine_piece, :], ts2.at[o], tr2.at[0], at_z(o))

    def a1_to_z(o):
        return remote(a1t.at[own, :], a1t.at[own, :], as2.at[o], ar2.at[0], at_z(o))

    t1_gather = [
        remote(t1.at[mine_piece, :], t1.at[mine_piece, :], ts3.at[o], tr3.at[o], at_q(o)) for o in range(1, Q)
    ]
    a1_gather = [remote(a1t.at[own, :], a1t.at[own, :], as3.at[o], ar3.at[o], at_x(o)) for o in range(1, nx)]
    lead_t = pltpu.make_async_copy(t_ref.at[mine_piece, :], t1.at[mine_piece, :], load_sem.at[2])
    lead_a = pltpu.make_async_copy(pt_ref.at[:, lead_cols], a1t.at[own, :], load_sem.at[3])

    @pl.when(root)
    def _():
        for o in range(1, Q):
            a1_to_q(o).start()
        lead_a.start()
        lead_t.start()
        for o in range(1, Q):
            t1_to_q(o).start()

    load_t.wait()
    thi[...] = t[...].astype(BF16)
    tlo[...] = (t[...] - thi[...].astype(F32)).astype(BF16)
    load_a.wait()
    product(0)

    sent(near_first)
    start(near_rest[:2])
    arrive(near_first[:2])
    start(onward[:2])
    start(near_rest[2:])
    arrive(near_first[2:])

    def reduce_start(source, buf, ss, rs, rows, peers, index):
        out = []
        for o in range(1, peers[0]):
            part = pl.ds(pl.multiple_of(index(o) * rows, rows), rows)
            out.append(remote(source.at[part, :], buf.at[o], ss.at[o], rs.at[o], peers[1](o)))
        return out

    gp = x * ny + y
    gpart = N // (nx * ny)
    mine_g = pl.ds(pl.multiple_of(gp * gpart, gpart), gpart)
    zc = z * 2 + core
    g1 = reduce_start(
        g, gslots, gs1, gr1, gpart, (nx * ny, at_xy), lambda o: along_x(o // ny) * ny + along_y(o % ny)
    )
    g2 = [remote(gz.at[zc], gz.at[zc], gs2.at[o], gr2.at[o], at_zc(o)) for o in range(1, 2 * nz)]
    g3 = [remote(gsum.at[mine_g, :], gsum.at[mine_g, :], gs3.at[o], gr3.at[o], at_xy(o)) for o in range(1, nx * ny)]

    part = at[:, columns(x)]
    g[...] = dot(part, part, ((1,), (1,)), HIGH)
    start(g1)
    arrive(near_rest[:2])
    start(onward[2:])

    @pl.when(root)
    def _():
        lead_a.wait()

    @pl.when(first & jnp.logical_not(root))
    def _():
        a1_to_q(1).wait_recv()

    @pl.when(first)
    def _():
        for o in range(1, nz):
            a1_to_z(o).start()

    sum_scattered(0)
    arrive(g1)
    total = g[mine_g, :]
    for o in range(1, nx * ny):
        total = total + gslots[o]
    gz[zc] = total
    start(g2)

    @pl.when(jnp.logical_not(first))
    def _():
        a1_to_z(1).wait_recv()

    start(a1_gather)

    @pl.when(root)
    def _():
        lead_t.wait()

    @pl.when(first & jnp.logical_not(root))
    def _():
        t1_to_q(1).wait_recv()

    @pl.when(first)
    def _():
        for o in range(1, nz):
            t1_to_z(o).start()

    arrive(near_rest[2:])
    product(1)
    sum_exchanged(0)
    arrive(g2)
    total = gz[0]
    for o in range(1, 2 * nz):
        total = total + gz[o]
    gsum[mine_g, :] = total
    start(g3)
    arrive(onward)
    product(2)
    sum_scattered(1)
    for i in range(0, at.shape[1], N):
        hi, lo = split(at[:, i : i + N].T)
        ahi_out[i : i + N, :] = hi
        alo_out[i : i + N, :] = lo
    sum_scattered(2)
    arrive(a1_gather)
    a1 = a1t[...].T
    row = lax.broadcasted_iota(jnp.int32, (N, N), 0)
    col = lax.broadcasted_iota(jnp.int32, (N, N), 1)
    m2[0:N, :] = a1
    m2[N : 2 * N, :] = jnp.where(row == col, 1.0, 0.0)
    arrive(g3)

    lane = lax.broadcasted_iota(jnp.int32, (8, N), 1)
    sub = lax.broadcasted_iota(jnp.int32, (8, N), 0)
    blocks = N // 8
    m1[...] = gsum[...]
    for b in range(blocks + 1):
        if b == 1:
            sum_exchanged(1)
        if b == 4:
            sum_exchanged(2)
        if b == 5:

            @pl.when(jnp.logical_not(first))
            def _():
                t1_to_z(1).wait_recv()

            start(t1_gather)
        if b == blocks:
            arrive(c3[0] + c3[1] + c3[2] + t1_gather)
            collect()
            d = dot3(rit[...], csum[...])
            d_out[...] = d
            t1x[...] = t1[...] - d
        steps, pivots = [], []
        if b < blocks:
            steps.append(eliminate(m1, b, False, pivots))
        if b > 0:
            steps.append(eliminate(m2, b - 1, True, []))
        interleave(*steps)
        if b < blocks:
            rows = slice(8 * b, 8 * b + 8)
            scale = lax.rsqrt(pivots[0])
            diagonal = sub + 8 * b
            block = m1[rows, :] * scale
            upper = jnp.where(lane >= diagonal, block, 0.0)
            inverse = jnp.where(lane < diagonal, block, jnp.where(lane == diagonal, scale, 0.0))
            lead = a1[8 * b : 8 * b + 8, :]
            diag = jnp.sum(lead * inverse, axis=1, keepdims=True)
            sign = jnp.where(diag >= 0, -1.0, 1.0)
            signed = sign * upper
            r_out[rows, :] = signed
            rit[rows, :] = sign * inverse
            bmat[rows, :] = lead - signed
            m2[rows, :] = m2[rows, :] - signed
    v = jnp.where(row <= col, m2[N : 2 * N, :], 0.0)
    linv = jnp.where(row == col, 1.0, jnp.where(row > col, m2[0:N, :], 0.0))
    khi, klo = split(dot3(v, dot3(linv, t1x[...])))
    khi_out[...] = khi
    klo_out[...] = klo
    vt = v.T
    m1[...] = vt
    vxt_out[...] = m1[own, :]
    l1t = jnp.where(row == col, 1.0, jnp.where(row < col, dot(vt, bmat[...], ((1,), (1,)), HIGH), 0.0))
    m1[...] = l1t
    l1xt_out[...] = m1[own, :]
    sent(near_rest + onward + g1 + g2 + g3)
    for h in range(3):
        sent(c1[h] + c2[h] + c3[h])
    sent(t1_gather + a1_gather)

    @pl.when(root)
    def _():
        sent([t1_to_q(o) for o in range(1, Q)])
        sent([a1_to_q(o) for o in range(1, Q)])

    @pl.when(first)
    def _():
        sent([t1_to_z(o) for o in range(1, nz)])
        sent([a1_to_z(o) for o in range(1, nz)])


def update_kernel(
    t_ref, ahi_ref, alo_ref, khi_ref, klo_ref, d_ref, vxt_ref, l1xt_ref, r_ref, out_ref, yt_ref, factor_ref, buf, yt, sems
):
    root = lax.axis_index("row") == 0
    nt = ((1,), (1,))
    rows = t_ref.shape[0]
    copies = [pltpu.make_async_copy(r_ref, factor_ref, sems.at[0])]
    copies[0].start()
    khi, klo = khi_ref[...], klo_ref[...]
    k2 = jnp.concatenate([khi, khi], axis=0)
    chunk = 256
    for i in range(rows // chunk):
        part = slice(i * chunk, (i + 1) * chunk)
        ahi, alo = ahi_ref[part, :], alo_ref[part, :]
        a2 = jnp.concatenate([ahi, alo], axis=1)
        buf[part, :] = t_ref[part, :] - (dot(a2, k2) + dot(ahi, klo))
        if i == 0:

            @pl.when(root)
            def _():
                buf[0:N, :] = d_ref[...]

        copies.append(pltpu.make_async_copy(buf.at[part, :], out_ref.at[part, :], sems.at[i + 1]))
        copies[-1].start()
        if i == rows // chunk - 3:
            vhi, vlo = split(vxt_ref[...])
            ahi, alo = ahi_ref[...], alo_ref[...]
            yt[...] = dot(vhi, ahi, nt) + dot(vhi, alo, nt) + dot(vlo, ahi, nt)

            @pl.when(root)
            def _():
                yt[:, 0:N] = l1xt_ref[...]

            copies.append(pltpu.make_async_copy(yt, yt_ref, sems.at[rows // chunk + 1]))
            copies[-1].start()
    for copy in copies:
        copy.wait()


def per_device(nz, nx, panel_block, trailing):
    rows, cols = trailing.shape
    w = N // nx
    dma = pltpu.SemaphoreType.DMA
    any_spec = pl.BlockSpec(memory_space=pltpu.HBM)
    vmem = pl.BlockSpec(memory_space=pltpu.VMEM)
    hbm = functools.partial(pltpu.with_memory_space_constraint, memory_space=pltpu.HBM)
    shape = jax.ShapeDtypeStruct
    ahi, alo, khi, klo, d, vxt, l1xt, factor = pl.pallas_call(
        functools.partial(factor_kernel, nz, nx),
        out_shape=[
            shape((rows, N), BF16), shape((rows, N), BF16), shape((N, cols), BF16), shape((N, cols), BF16), shape((N, cols), F32),
            shape((w, N), F32), shape((w, N), F32), shape((N, N), F32),
        ],
        in_specs=[any_spec, any_spec],
        out_specs=[vmem] * 8,
        scratch_shapes=[
            pltpu.VMEM((N, rows), F32), pltpu.VMEM((rows, cols), F32), pltpu.VMEM((rows, cols), BF16),
            pltpu.VMEM((rows, cols), BF16), pltpu.VMEM((N, N), F32), pltpu.VMEM((N, cols), F32),
            pltpu.VMEM((N, N), F32), pltpu.VMEM((16, 8, N), F32), pltpu.VMEM((2 * nz, 8, N), F32), pltpu.VMEM((N, N), F32),
            pltpu.VMEM((2 * w, cols), F32), pltpu.VMEM((N, cols), F32),
            pltpu.VMEM((N, N), F32), pltpu.VMEM((2 * N, N), F32), pltpu.VMEM((N, N), F32), pltpu.VMEM((N, N), F32),
            pltpu.VMEM((N, cols), F32),
        ] + [pltpu.VMEM((count, w * wide // Q, cols), F32) for count in (Q, Q, nz, Q) for wide in (1, 2, 1)] + [
            dma((4,)), dma((13,)), dma((13,)),
        ] + [dma((16,))] * 6 + [dma((3, 8))] * 6 + [
            dma((8,)), dma((1,)), dma((8,)), dma((1,)), dma((8,)), dma((8,)),
            dma((8,)), dma((1,)), dma((8,)), dma((1,)), dma((nx,)), dma((nx,)),
        ],
        compiler_params=pltpu.CompilerParams(
            collective_id=0, has_side_effects=True, vmem_limit_bytes=48 * 1024 * 1024
        ),
        name="factor",
    )(hbm(panel_block.T), hbm(trailing))
    updated, yt, factor = pl.pallas_call(
        update_kernel,
        out_shape=[shape((rows, cols), F32), shape((w, rows), F32), shape((N, N), F32)],
        in_specs=[vmem] * 9,
        out_specs=[any_spec] * 3,
        scratch_shapes=[pltpu.VMEM((rows, cols), F32), pltpu.VMEM((w, rows), F32), dma((rows // 256 + 2,))],
        compiler_params=pltpu.CompilerParams(vmem_limit_bytes=32 * 1024 * 1024),
        name="update",
    )(trailing, ahi, alo, khi, klo, d, vxt, l1xt, factor)
    return updated, yt.T, factor


def solution(mesh):
    nz, nx = mesh.shape["row"] // Q, mesh.shape["col"]
    in_specs = (P("row", "col"), P("row", "col"))
    out_specs = (P("row", "col"), P("row", "col"), P())
    return jax.shard_map(
        functools.partial(per_device, nz, nx), mesh=mesh, in_specs=in_specs, out_specs=out_specs, check_vma=False
    )
```

```python
import functools

import jax
import jax.numpy as jnp
from jax import lax
from jax.experimental import pallas as pl
from jax.experimental.pallas import tpu as pltpu
from jax.sharding import PartitionSpec as P

F32 = jnp.float32
BF16 = jnp.bfloat16
HIGH = lax.Precision.HIGHEST
N = 128
Q = 8


def dot(a, b, dims=((1,), (0,)), precision=None):
    return lax.dot_general(a, b, (dims, ((), ())), precision=precision, preferred_element_type=F32)


def split(x):
    hi = x.astype(BF16)
    return hi, (x - hi.astype(F32)).astype(BF16)


def dot3(a, b):
    (ah, al), (bh, bl) = split(a), split(b)
    return dot(ah, bh) + (dot(ah, bl) + dot(al, bh))


def eliminate(m_ref, b, bottom, out):
    r0 = 8 * b
    lane = lax.broadcasted_iota(jnp.int32, (8, N), 1)
    sub = lax.broadcasted_iota(jnp.int32, (8, N), 0)
    parts = []
    if r0 + 8 < N:
        parts.append((r0 + 8, N - r0 - 8, False))
    if bottom:
        parts.append((N, r0 + 8, True))
    rows = m_ref[r0 : r0 + 8, :]
    rest = [m_ref[s : s + n, :] for s, n, _ in parts]
    cols = [
        [jnp.broadcast_to(p[:, r0 + j : r0 + j + 1], (p.shape[0], N)) for j in range(8)]
        for p in [rows] + rest
    ]
    mults, pivots = [], None
    for k in range(8):
        yield
        c0 = cols[0][k]
        d = jnp.broadcast_to(c0[k : k + 1, :], (8, N))
        inv = 1.0 / d
        pivots = d if pivots is None else jnp.where(sub == k, d, pivots)
        ms = [jnp.where(sub > k, c0 * inv, 0.0)] + [c[k] * inv[0:1, :] for c in cols[1:]]
        mults.append(ms)
        for j in range(k + 1, 8):
            top = cols[0][j][k : k + 1, :]
            for i in range(len(cols)):
                cols[i][j] = cols[i][j] - ms[i] * top
    pivot_rows = []
    for k in range(8):
        lk = r0 + k
        row = jnp.where(lane[0:1] == lk, 1.0, rows[k : k + 1, :])
        rows = jnp.where((lane == lk) & (sub > k), 0.0, rows) - mults[k][0] * row
        pivot_rows.append(jnp.where((lane[0:1] > lk) & (lane[0:1] < r0 + 8), 0.0, row))
    for i, (s, n, low) in enumerate(parts):
        lane_n = lax.broadcasted_iota(jnp.int32, (n, N), 1)
        acc = jnp.where((lane_n >= r0) & (lane_n < r0 + 8), 0.0, rest[i])
        for k in range(8):
            row = jnp.where(lane[0:1] >= r0 + 8, pivot_rows[k], 0.0) if low else pivot_rows[k]
            acc = acc - mults[k][i + 1] * row
        if low:
            for k in range(8):
                acc = jnp.where(lane_n == r0 + k, mults[k][i + 1], acc)
        m_ref[s : s + n, :] = acc
    m_ref[r0 : r0 + 8, :] = rows
    out.append(pivots)


def interleave(*steps):
    steps = list(steps)
    while steps:
        for step in list(steps):
            if next(step, True) is True:
                steps.remove(step)


def remote(src, dst, send, recv, device):
    return pltpu.make_async_remote_copy(
        src_ref=src, dst_ref=dst, send_sem=send, recv_sem=recv, device_id=device, device_id_type=pl.DeviceIdType.MESH
    )


def factor_kernel(
    nz, nx,
    pt_ref, t_ref,
    ahi_out, alo_out, khi_out, klo_out, d_out, vxt_out, l1xt_out, r_out, t,
    at, thi, tlo, a1t, t1, g, gslots, gz, gsum, strips, csum, m1, m2, rit, bmat, p0, p1, s0, s1, z0, z1, e0, e1,
    load_sem, xs, xr, gs1, gr1, gs2, gr2, gs3, gr3, cs1, cr1, cs2, cr2, cs3, cr3, ts1, tr1, ts2, tr2, ts3, tr3,
    as1, ar1, as2, ar2, as3, ar3,
):
    cparts, cslots, cz, call = (p0, p1), (s0, s1), (z0, z1), (e0, e1)
    r = lax.axis_index("row")
    x = lax.axis_index("col")
    z, q = lax.div(r, Q), lax.rem(r, Q)
    ny = Q // 2
    y, core = lax.div(q, 2), lax.rem(q, 2)
    w = N // nx
    seg = pt_ref.shape[1] // nx

    def along_x(o):
        return lax.rem(x + o, nx)

    def along_y(o):
        return lax.rem(y + o, ny)

    def at_x(o):
        return {"col": along_x(o)}

    def at_q(o):
        return {"row": z * Q + lax.rem(q + o, Q)}

    def at_z(o):
        return {"row": lax.rem(z + o, nz) * Q + q}

    def at_xy(o):
        return {"row": z * Q + along_y(o % ny) * 2 + core, "col": along_x(o // ny)}

    def at_zc(o):
        return {"row": lax.rem(z + o // 2, nz) * Q + y * 2 + lax.rem(core + o % 2, 2)}

    load_t = pltpu.make_async_copy(t_ref, t, load_sem.at[0])
    load_t.start()
    own = pl.ds(pl.multiple_of(x * w, w), w)
    load_a = pltpu.make_async_copy(pt_ref, at.at[own, :], load_sem.at[1])
    load_a.start()

    barrier = pltpu.get_barrier_semaphore()
    greeted = [at_xy(o) for o in range(1, nx * ny)] + [at_zc(o) for o in range(1, 2 * nz)]
    greeted += [{"row": z * Q + along_y(o) * 2 + (1 - core)} for o in range(1, ny)]
    for device in greeted:
        pl.semaphore_signal(barrier, inc=1, device_id=device, device_id_type=pl.DeviceIdType.MESH)
    pl.semaphore_wait(barrier, len(greeted))

    def columns(s):
        return pl.ds(pl.multiple_of(s * seg, seg), seg)

    def strip(owner, cols):
        return at.at[pl.ds(pl.multiple_of(owner * w, w), w), cols]

    def tell(i, o, s):
        return remote(pt_ref.at[:, columns(s)], strip(x, columns(s)), xs.at[i], xr.at[i], at_x(o))

    def forward(i, o, owner, cols):
        return remote(strip(owner, cols), strip(owner, cols), xs.at[i], xr.at[i], at_x(o))

    xp, xm, x2 = along_x(1), along_x(nx - 1), along_x(2)
    plus, minus = 1, nx - 1
    first_half = pl.ds(pl.multiple_of(xm * seg, seg), seg // 2)
    second_half = pl.ds(pl.multiple_of(xp * seg + seg // 2, seg // 2), seg // 2)
    near_first = [tell(0, plus, xp), tell(1, minus, xm), tell(2, 2, x2)]
    near_rest = [
        tell(3, plus, x), tell(4, minus, x), tell(5, plus, x2), tell(6, minus, x2), tell(7, plus, xm), tell(8, minus, xp),
    ]
    onward = [
        forward(9, plus, xm, columns(x)), forward(10, minus, xp, columns(x)),
        forward(11, plus, xm, first_half), forward(12, minus, xp, second_half),
    ]

    def start(copies):
        for copy in copies:
            copy.start()

    def arrive(copies):
        for copy in copies:
            copy.wait_recv()

    def sent(copies):
        for copy in copies:
            copy.wait_send()

    start(near_first)

    owners = [[x, xp, xm], [x2]]
    c1, c2, c3 = [], [], []
    for h in range(2):
        c1.append([
            remote(cparts[h].at[lax.rem(q + o, Q)], cslots[h].at[o], cs1.at[h, o], cr1.at[h, o], at_q(o))
            for o in range(1, Q)
        ])
        c2.append([remote(cz[h].at[z], cz[h].at[z], cs2.at[h, o], cr2.at[h, o], at_z(o)) for o in range(1, nz)])
        c3.append([remote(call[h].at[q], call[h].at[q], cs3.at[h, o], cr3.at[h, o], at_q(o)) for o in range(1, Q)])

    def product(h):
        rows = len(owners[h]) * w
        n = rows // Q
        pieces = [split(at[pl.ds(pl.multiple_of(owner * w, w), w), :]) for owner in owners[h]]
        hi = jnp.concatenate([p[0] for p in pieces], axis=0)
        lo = jnp.concatenate([p[1] for p in pieces], axis=0)
        both = dot(jnp.concatenate([hi, lo], axis=0), thi[...])
        strips[0:rows, :] = both[:rows] + both[rows:] + dot(hi, tlo[...])
        for j in range(Q):
            cparts[h][j] = strips[j * n : (j + 1) * n, :]
        start(c1[h])

    def sum_scattered(h):
        arrive(c1[h])
        total = cparts[h][q]
        for o in range(1, Q):
            total = total + cslots[h][o]
        cz[h][z] = total
        start(c2[h])

    def sum_exchanged(h):
        arrive(c2[h])
        total = cz[h][0]
        for o in range(1, nz):
            total = total + cz[h][o]
        call[h][q] = total
        start(c3[h])

    def collect(h):
        n = len(owners[h]) * w // Q
        for j in range(Q):
            strips[j * n : (j + 1) * n, :] = call[h][j]
        for i, owner in enumerate(owners[h]):
            csum[pl.ds(pl.multiple_of(owner * w, w), w), :] = strips[i * w : (i + 1) * w, :]

    root = r == 0
    first = z == 0
    piece = N // Q
    mine_piece = pl.ds(pl.multiple_of(q * piece, piece), piece)
    lead_cols = pl.ds(0, N)

    def t1_to_q(o):
        rows = pl.ds(pl.multiple_of(lax.rem(q + o, Q) * piece, piece), piece)
        return remote(t_ref.at[rows, :], t1.at[rows, :], ts1.at[o], tr1.at[0], at_q(o))

    def a1_to_q(o):
        return remote(pt_ref.at[:, lead_cols], a1t.at[own, :], as1.at[o], ar1.at[0], at_q(o))

    def t1_to_z(o):
        return remote(t1.at[mine_piece, :], t1.at[mine_piece, :], ts2.at[o], tr2.at[0], at_z(o))

    def a1_to_z(o):
        return remote(a1t.at[own, :], a1t.at[own, :], as2.at[o], ar2.at[0], at_z(o))

    t1_gather = [
        remote(t1.at[mine_piece, :], t1.at[mine_piece, :], ts3.at[o], tr3.at[o], at_q(o)) for o in range(1, Q)
    ]
    a1_gather = [remote(a1t.at[own, :], a1t.at[own, :], as3.at[o], ar3.at[o], at_x(o)) for o in range(1, nx)]
    lead_t = pltpu.make_async_copy(t_ref.at[mine_piece, :], t1.at[mine_piece, :], load_sem.at[2])
    lead_a = pltpu.make_async_copy(pt_ref.at[:, lead_cols], a1t.at[own, :], load_sem.at[3])

    @pl.when(root)
    def _():
        for o in range(1, Q):
            a1_to_q(o).start()
        lead_a.start()
        lead_t.start()
        for o in range(1, Q):
            t1_to_q(o).start()

    load_t.wait()
    thi[...] = t[...].astype(BF16)
    tlo[...] = (t[...] - thi[...].astype(F32)).astype(BF16)
    load_a.wait()

    sent(near_first)
    start(near_rest[:2])
    arrive(near_first[:2])
    start(onward[:2])
    start(near_rest[2:])
    arrive(near_first[2:])

    def reduce_start(source, buf, ss, rs, rows, peers, index):
        out = []
        for o in range(1, peers[0]):
            part = pl.ds(pl.multiple_of(index(o) * rows, rows), rows)
            out.append(remote(source.at[part, :], buf.at[o], ss.at[o], rs.at[o], peers[1](o)))
        return out

    gp = x * ny + y
    gpart = N // (nx * ny)
    mine_g = pl.ds(pl.multiple_of(gp * gpart, gpart), gpart)
    zc = z * 2 + core
    g1 = reduce_start(
        g, gslots, gs1, gr1, gpart, (nx * ny, at_xy), lambda o: along_x(o // ny) * ny + along_y(o % ny)
    )
    g2 = [remote(gz.at[zc], gz.at[zc], gs2.at[o], gr2.at[o], at_zc(o)) for o in range(1, 2 * nz)]
    g3 = [remote(gsum.at[mine_g, :], gsum.at[mine_g, :], gs3.at[o], gr3.at[o], at_xy(o)) for o in range(1, nx * ny)]

    part = at[:, columns(x)]
    g[...] = dot(part, part, ((1,), (1,)), HIGH)
    start(g1)
    arrive(near_rest[:2])
    start(onward[2:])

    @pl.when(root)
    def _():
        lead_a.wait()

    @pl.when(first & jnp.logical_not(root))
    def _():
        a1_to_q(1).wait_recv()

    @pl.when(first)
    def _():
        for o in range(1, nz):
            a1_to_z(o).start()

    arrive(g1)
    total = g[mine_g, :]
    for o in range(1, nx * ny):
        total = total + gslots[o]
    gz[zc] = total
    start(g2)

    @pl.when(jnp.logical_not(first))
    def _():
        a1_to_z(1).wait_recv()

    start(a1_gather)

    @pl.when(root)
    def _():
        lead_t.wait()

    @pl.when(first & jnp.logical_not(root))
    def _():
        t1_to_q(1).wait_recv()

    @pl.when(first)
    def _():
        for o in range(1, nz):
            t1_to_z(o).start()

    arrive(near_rest[2:])
    product(0)
    arrive(g2)
    total = gz[0]
    for o in range(1, 2 * nz):
        total = total + gz[o]
    gsum[mine_g, :] = total
    start(g3)
    arrive(onward)
    product(1)
    sum_scattered(0)
    for i in range(0, at.shape[1], N):
        hi, lo = split(at[:, i : i + N].T)
        ahi_out[i : i + N, :] = hi
        alo_out[i : i + N, :] = lo
    arrive(a1_gather)
    a1 = a1t[...].T
    row = lax.broadcasted_iota(jnp.int32, (N, N), 0)
    col = lax.broadcasted_iota(jnp.int32, (N, N), 1)
    m2[0:N, :] = a1
    m2[N : 2 * N, :] = jnp.where(row == col, 1.0, 0.0)
    arrive(g3)

    lane = lax.broadcasted_iota(jnp.int32, (8, N), 1)
    sub = lax.broadcasted_iota(jnp.int32, (8, N), 0)
    blocks = N // 8
    m1[...] = gsum[...]
    for b in range(blocks + 1):
        if b == 3:
            sum_scattered(1)
        if b == 9:
            sum_exchanged(0)
        if b == 13:
            sum_exchanged(1)
        if b == 5:

            @pl.when(jnp.logical_not(first))
            def _():
                t1_to_z(1).wait_recv()

            start(t1_gather)
        steps, pivots = [], []
        if b < blocks:
            steps.append(eliminate(m1, b, False, pivots))
        if b > 0:
            steps.append(eliminate(m2, b - 1, True, []))
        interleave(*steps)
        if b < blocks:
            rows = slice(8 * b, 8 * b + 8)
            scale = lax.rsqrt(pivots[0])
            diagonal = sub + 8 * b
            block = m1[rows, :] * scale
            upper = jnp.where(lane >= diagonal, block, 0.0)
            inverse = jnp.where(lane < diagonal, block, jnp.where(lane == diagonal, scale, 0.0))
            lead = a1[8 * b : 8 * b + 8, :]
            diag = jnp.sum(lead * inverse, axis=1, keepdims=True)
            sign = jnp.where(diag >= 0, -1.0, 1.0)
            signed = sign * upper
            r_out[rows, :] = signed
            rit[rows, :] = sign * inverse
            bmat[rows, :] = lead - signed
            m2[rows, :] = m2[rows, :] - signed
    v = jnp.where(row <= col, m2[N : 2 * N, :], 0.0)
    linv = jnp.where(row == col, 1.0, jnp.where(row > col, m2[0:N, :], 0.0))
    vt = v.T
    m1[...] = vt
    vxt_out[...] = m1[own, :]
    l1t = jnp.where(row == col, 1.0, jnp.where(row < col, dot(vt, bmat[...], ((1,), (1,)), HIGH), 0.0))
    m1[...] = l1t
    l1xt_out[...] = m1[own, :]
    inv = dot3(v, linv)
    weight = dot3(inv, rit[...])
    arrive(t1_gather)
    known = dot3(inv, t1[...])
    sent(near_rest + onward + g1 + g2 + g3 + c1[0] + c1[1] + c2[0] + t1_gather + a1_gather)

    @pl.when(root)
    def _():
        sent([t1_to_q(o) for o in range(1, Q)])
        sent([a1_to_q(o) for o in range(1, Q)])

    @pl.when(first)
    def _():
        sent([t1_to_z(o) for o in range(1, nz)])
        sent([a1_to_z(o) for o in range(1, nz)])

    arrive(c3[0])
    collect(0)
    sent(c2[1])
    arrive(c3[1])
    collect(1)
    chi, clo = split(csum[...])
    both = jnp.concatenate([weight, rit[...]], axis=0)
    bhi, blo = split(both)
    both = dot(bhi, chi) + (dot(bhi, clo) + dot(blo, chi))
    khi, klo = split(known - both[:N])
    khi_out[...] = khi
    klo_out[...] = klo
    d_out[...] = both[N:]
    sent(c3[0] + c3[1])


def update_kernel(
    t_ref, ahi_ref, alo_ref, khi_ref, klo_ref, d_ref, vxt_ref, l1xt_ref, r_ref, out_ref, yt_ref, factor_ref, buf, yt, sems
):
    root = lax.axis_index("row") == 0
    nt = ((1,), (1,))
    rows = t_ref.shape[0]
    copies = [pltpu.make_async_copy(r_ref, factor_ref, sems.at[0])]
    copies[0].start()
    khi, klo = khi_ref[...], klo_ref[...]
    k2 = jnp.concatenate([khi, khi], axis=0)
    chunk = 256
    for i in range(rows // chunk):
        part = slice(i * chunk, (i + 1) * chunk)
        ahi, alo = ahi_ref[part, :], alo_ref[part, :]
        a2 = jnp.concatenate([ahi, alo], axis=1)
        buf[part, :] = t_ref[part, :] - (dot(a2, k2) + dot(ahi, klo))
        if i == 0:

            @pl.when(root)
            def _():
                buf[0:N, :] = d_ref[...]

        copies.append(pltpu.make_async_copy(buf.at[part, :], out_ref.at[part, :], sems.at[i + 1]))
        copies[-1].start()
        if i == rows // chunk - 3:
            vhi, vlo = split(vxt_ref[...])
            ahi, alo = ahi_ref[...], alo_ref[...]
            yt[...] = dot(vhi, ahi, nt) + dot(vhi, alo, nt) + dot(vlo, ahi, nt)

            @pl.when(root)
            def _():
                yt[:, 0:N] = l1xt_ref[...]

            copies.append(pltpu.make_async_copy(yt, yt_ref, sems.at[rows // chunk + 1]))
            copies[-1].start()
    for copy in copies:
        copy.wait()


def per_device(nz, nx, panel_block, trailing):
    rows, cols = trailing.shape
    w = N // nx
    dma = pltpu.SemaphoreType.DMA
    any_spec = pl.BlockSpec(memory_space=pltpu.HBM)
    vmem = pl.BlockSpec(memory_space=pltpu.VMEM)
    hbm = functools.partial(pltpu.with_memory_space_constraint, memory_space=pltpu.HBM)
    shape = jax.ShapeDtypeStruct
    ahi, alo, khi, klo, d, vxt, l1xt, factor, held = pl.pallas_call(
        functools.partial(factor_kernel, nz, nx),
        out_shape=[
            shape((rows, N), BF16), shape((rows, N), BF16), shape((N, cols), BF16), shape((N, cols), BF16), shape((N, cols), F32),
            shape((w, N), F32), shape((w, N), F32), shape((N, N), F32), shape((rows, cols), F32),
        ],
        in_specs=[any_spec, any_spec],
        out_specs=[vmem] * 9,
        scratch_shapes=[
            pltpu.VMEM((N, rows), F32), pltpu.VMEM((rows, cols), BF16),
            pltpu.VMEM((rows, cols), BF16), pltpu.VMEM((N, N), F32), pltpu.VMEM((N, cols), F32),
            pltpu.VMEM((N, N), F32), pltpu.VMEM((16, 8, N), F32), pltpu.VMEM((2 * nz, 8, N), F32), pltpu.VMEM((N, N), F32),
            pltpu.VMEM((3 * w, cols), F32), pltpu.VMEM((N, cols), F32),
            pltpu.VMEM((N, N), F32), pltpu.VMEM((2 * N, N), F32), pltpu.VMEM((N, N), F32), pltpu.VMEM((N, N), F32),
        ] + [pltpu.VMEM((count, w * wide // Q, cols), F32) for count in (Q, Q, nz, Q) for wide in (3, 1)] + [
            dma((4,)), dma((13,)), dma((13,)),
        ] + [dma((16,))] * 6 + [dma((2, 8))] * 6 + [
            dma((8,)), dma((1,)), dma((8,)), dma((1,)), dma((8,)), dma((8,)),
            dma((8,)), dma((1,)), dma((8,)), dma((1,)), dma((nx,)), dma((nx,)),
        ],
        compiler_params=pltpu.CompilerParams(
            collective_id=0, has_side_effects=True, vmem_limit_bytes=48 * 1024 * 1024
        ),
        name="factor",
    )(hbm(panel_block.T), hbm(trailing))
    updated, yt, factor = pl.pallas_call(
        update_kernel,
        out_shape=[shape((rows, cols), F32), shape((w, rows), F32), shape((N, N), F32)],
        in_specs=[vmem] * 9,
        out_specs=[any_spec] * 3,
        scratch_shapes=[pltpu.VMEM((rows, cols), F32), pltpu.VMEM((w, rows), F32), dma((rows // 256 + 2,))],
        compiler_params=pltpu.CompilerParams(vmem_limit_bytes=32 * 1024 * 1024),
        name="update",
    )(held, ahi, alo, khi, klo, d, vxt, l1xt, factor)
    return updated, yt.T, factor


def solution(mesh):
    nz, nx = mesh.shape["row"] // Q, mesh.shape["col"]
    in_specs = (P("row", "col"), P("row", "col"))
    out_specs = (P("row", "col"), P("row", "col"), P())
    return jax.shard_map(
        functools.partial(per_device, nz, nx), mesh=mesh, in_specs=in_specs, out_specs=out_specs, check_vma=False
    )
```

```python
import functools

import jax
import jax.numpy as jnp
from jax import lax
from jax.experimental import pallas as pl
from jax.experimental.pallas import tpu as pltpu
from jax.sharding import PartitionSpec as P

F32 = jnp.float32
BF16 = jnp.bfloat16
HIGH = lax.Precision.HIGHEST
N = 128
Q = 8


def dot(a, b, dims=((1,), (0,)), precision=None):
    return lax.dot_general(a, b, (dims, ((), ())), precision=precision, preferred_element_type=F32)


def split(x):
    hi = x.astype(BF16)
    return hi, (x - hi.astype(F32)).astype(BF16)


def dot3(a, b):
    (ah, al), (bh, bl) = split(a), split(b)
    return dot(ah, bh) + (dot(ah, bl) + dot(al, bh))


def eliminate(m_ref, b, bottom, out):
    r0 = 8 * b
    lane = lax.broadcasted_iota(jnp.int32, (8, N), 1)
    sub = lax.broadcasted_iota(jnp.int32, (8, N), 0)
    parts = []
    if r0 + 8 < N:
        parts.append((r0 + 8, N - r0 - 8, False))
    if bottom:
        parts.append((N, r0 + 8, True))
    rows = m_ref[r0 : r0 + 8, :]
    rest = [m_ref[s : s + n, :] for s, n, _ in parts]
    cols = [
        [jnp.broadcast_to(p[:, r0 + j : r0 + j + 1], (p.shape[0], N)) for j in range(8)]
        for p in [rows] + rest
    ]
    mults, pivots = [], None
    for k in range(8):
        yield
        c0 = cols[0][k]
        d = jnp.broadcast_to(c0[k : k + 1, :], (8, N))
        inv = 1.0 / d
        pivots = d if pivots is None else jnp.where(sub == k, d, pivots)
        ms = [jnp.where(sub > k, c0 * inv, 0.0)] + [c[k] * inv[0:1, :] for c in cols[1:]]
        mults.append(ms)
        for j in range(k + 1, 8):
            top = cols[0][j][k : k + 1, :]
            for i in range(len(cols)):
                cols[i][j] = cols[i][j] - ms[i] * top
    pivot_rows = []
    for k in range(8):
        lk = r0 + k
        row = jnp.where(lane[0:1] == lk, 1.0, rows[k : k + 1, :])
        rows = jnp.where((lane == lk) & (sub > k), 0.0, rows) - mults[k][0] * row
        pivot_rows.append(jnp.where((lane[0:1] > lk) & (lane[0:1] < r0 + 8), 0.0, row))
    for i, (s, n, low) in enumerate(parts):
        lane_n = lax.broadcasted_iota(jnp.int32, (n, N), 1)
        acc = jnp.where((lane_n >= r0) & (lane_n < r0 + 8), 0.0, rest[i])
        for k in range(8):
            row = jnp.where(lane[0:1] >= r0 + 8, pivot_rows[k], 0.0) if low else pivot_rows[k]
            acc = acc - mults[k][i + 1] * row
        if low:
            for k in range(8):
                acc = jnp.where(lane_n == r0 + k, mults[k][i + 1], acc)
        m_ref[s : s + n, :] = acc
    m_ref[r0 : r0 + 8, :] = rows
    out.append(pivots)


def interleave(*steps):
    steps = list(steps)
    while steps:
        for step in list(steps):
            if next(step, True) is True:
                steps.remove(step)


def remote(src, dst, send, recv, device):
    return pltpu.make_async_remote_copy(
        src_ref=src, dst_ref=dst, send_sem=send, recv_sem=recv, device_id=device, device_id_type=pl.DeviceIdType.MESH
    )


def factor_kernel(
    nz, nx,
    pt_ref, t_ref,
    ahi_out, alo_out, khi_out, klo_out, d_out, vxt_out, l1xt_out, r_out, t,
    at, thi, tlo, a1t, t1, g, gslots, gz, gsum, strips, csum, m1, m2, rit, bmat, p0, p1, s0, s1, z0, z1, e0, e1,
    load_sem, ss, rs,
):
    cparts, cslots, cz, call = (p0, p1), (s0, s1), (z0, z1), (e0, e1)
    r = lax.axis_index("row")
    x = lax.axis_index("col")
    z, q = lax.div(r, Q), lax.rem(r, Q)
    ny = Q // 2
    y, core = lax.div(q, 2), lax.rem(q, 2)
    w = N // nx
    seg = pt_ref.shape[1] // nx

    def along_x(o):
        return lax.rem(x + o, nx)

    def along_y(o):
        return lax.rem(y + o, ny)

    def at_x(o):
        return {"col": along_x(o)}

    def at_q(o):
        return {"row": z * Q + lax.rem(q + o, Q)}

    def at_z(o):
        return {"row": lax.rem(z + o, nz) * Q + q}

    def at_xy(o):
        return {"row": z * Q + along_y(o % ny) * 2 + core, "col": along_x(o // ny)}

    def at_zc(o):
        return {"row": lax.rem(z + o // 2, nz) * Q + y * 2 + lax.rem(core + o % 2, 2)}

    load_t = pltpu.make_async_copy(t_ref, t, load_sem.at[0])
    load_t.start()
    own = pl.ds(pl.multiple_of(x * w, w), w)
    load_a = pltpu.make_async_copy(pt_ref, at.at[own, :], load_sem.at[1])
    load_a.start()

    barrier = pltpu.get_barrier_semaphore()
    greeted = [at_xy(o) for o in range(1, nx * ny)] + [at_zc(o) for o in range(1, 2 * nz)]
    greeted += [{"row": z * Q + along_y(o) * 2 + (1 - core)} for o in range(1, ny)]
    for device in greeted:
        pl.semaphore_signal(barrier, inc=1, device_id=device, device_id_type=pl.DeviceIdType.MESH)
    pl.semaphore_wait(barrier, len(greeted))

    def columns(s):
        return pl.ds(pl.multiple_of(s * seg, seg), seg)

    def strip(owner, cols):
        return at.at[pl.ds(pl.multiple_of(owner * w, w), w), cols]

    def tell(send, recv, o, s):
        return remote(pt_ref.at[:, columns(s)], strip(x, columns(s)), ss.at[send], rs.at[recv], at_x(o))

    def forward(o, owner, cols):
        return remote(strip(owner, cols), strip(owner, cols), ss.at[1], rs.at[4], at_x(o))

    def whole(i, ref, recv=None):
        return remote(ref, ref, ss.at[i], rs.at[i if recv is None else recv], at_x(1))

    xp, xm, x2 = along_x(1), along_x(nx - 1), along_x(2)
    plus, minus = 1, nx - 1
    first_half = pl.ds(pl.multiple_of(xm * seg, seg), seg // 2)
    second_half = pl.ds(pl.multiple_of(xp * seg + seg // 2, seg // 2), seg // 2)
    near_first = [tell(0, 0, plus, xp), tell(0, 0, minus, xm), tell(0, 1, 2, x2)]
    near_rest = [
        tell(1, 2, plus, x), tell(1, 2, minus, x),
        tell(1, 3, plus, x2), tell(1, 3, minus, x2), tell(1, 3, plus, xm), tell(1, 3, minus, xp),
    ]
    onward = [
        forward(plus, xm, columns(x)), forward(minus, xp, columns(x)),
        forward(plus, xm, first_half), forward(minus, xp, second_half),
    ]

    def units(n, m=1):
        return at.at[0 : n * w, 0 : m * seg]

    def start(copies):
        for copy in copies:
            copy.start()

    def arrive(i, ref):
        whole(i, ref, i).wait_recv()

    def sent(i, ref):
        whole(i, ref).wait_send()

    start(near_first)

    owners = [[x, xp, xm], [x2]]
    c1, c2, c3 = [], [], []
    for h in range(2):
        c1.append([
            remote(cparts[h].at[lax.rem(q + o, Q)], cslots[h].at[o], ss.at[8 + h], rs.at[8 + h], at_q(o))
            for o in range(1, Q)
        ])
        c2.append([remote(cz[h].at[z], cz[h].at[z], ss.at[10 + h], rs.at[10 + h], at_z(o)) for o in range(1, nz)])
        c3.append([remote(call[h].at[q], call[h].at[q], ss.at[12 + h], rs.at[12 + h], at_q(o)) for o in range(1, Q)])

    def product(h):
        rows = len(owners[h]) * w
        n = rows // Q
        pieces = [split(at[pl.ds(pl.multiple_of(owner * w, w), w), :]) for owner in owners[h]]
        hi = jnp.concatenate([p[0] for p in pieces], axis=0)
        lo = jnp.concatenate([p[1] for p in pieces], axis=0)
        both = dot(jnp.concatenate([hi, lo], axis=0), thi[...])
        strips[0:rows, :] = both[:rows] + both[rows:] + dot(hi, tlo[...])
        for j in range(Q):
            cparts[h][j] = strips[j * n : (j + 1) * n, :]
        start(c1[h])

    def sum_scattered(h):
        arrive(8 + h, cslots[h].at[1:Q])
        total = cparts[h][q]
        for o in range(1, Q):
            total = total + cslots[h][o]
        cz[h][z] = total
        start(c2[h])

    def sum_exchanged(h):
        arrive(10 + h, cz[h].at[1:nz])
        total = cz[h][0]
        for o in range(1, nz):
            total = total + cz[h][o]
        call[h][q] = total
        start(c3[h])

    def collect(h):
        n = len(owners[h]) * w // Q
        for j in range(Q):
            strips[j * n : (j + 1) * n, :] = call[h][j]
        for i, owner in enumerate(owners[h]):
            csum[pl.ds(pl.multiple_of(owner * w, w), w), :] = strips[i * w : (i + 1) * w, :]

    root = r == 0
    first = z == 0
    piece = N // Q
    mine_piece = pl.ds(pl.multiple_of(q * piece, piece), piece)
    lead_cols = pl.ds(0, N)

    def t1_to_q(o):
        rows = pl.ds(pl.multiple_of(lax.rem(q + o, Q) * piece, piece), piece)
        return remote(t_ref.at[rows, :], t1.at[rows, :], ss.at[14], rs.at[14], at_q(o))

    def a1_to_q(o):
        return remote(pt_ref.at[:, lead_cols], a1t.at[own, :], ss.at[17], rs.at[17], at_q(o))

    def t1_to_z(o):
        return remote(t1.at[mine_piece, :], t1.at[mine_piece, :], ss.at[15], rs.at[15], at_z(o))

    def a1_to_z(o):
        return remote(a1t.at[own, :], a1t.at[own, :], ss.at[18], rs.at[18], at_z(o))

    t1_gather = [
        remote(t1.at[mine_piece, :], t1.at[mine_piece, :], ss.at[16], rs.at[16], at_q(o)) for o in range(1, Q)
    ]
    a1_gather = [remote(a1t.at[own, :], a1t.at[own, :], ss.at[19], rs.at[19], at_x(o)) for o in range(1, nx)]
    lead_t = pltpu.make_async_copy(t_ref.at[mine_piece, :], t1.at[mine_piece, :], load_sem.at[2])
    lead_a = pltpu.make_async_copy(pt_ref.at[:, lead_cols], a1t.at[own, :], load_sem.at[3])

    @pl.when(root)
    def _():
        for o in range(1, Q):
            a1_to_q(o).start()
        lead_a.start()
        lead_t.start()
        for o in range(1, Q):
            t1_to_q(o).start()

    load_t.wait()
    thi[...] = t[...].astype(BF16)
    tlo[...] = (t[...] - thi[...].astype(F32)).astype(BF16)
    load_a.wait()

    sent(0, units(3))
    start(near_rest[:2])
    arrive(0, units(2))
    start(onward[:2])
    start(near_rest[2:])
    arrive(1, units(1))

    gp = x * ny + y
    gpart = N // (nx * ny)
    mine_g = pl.ds(pl.multiple_of(gp * gpart, gpart), gpart)
    zc = z * 2 + core
    g1 = []
    for o in range(1, nx * ny):
        there = pl.multiple_of((along_x(o // ny) * ny + along_y(o % ny)) * gpart, gpart)
        g1.append(remote(g.at[pl.ds(there, gpart), :], gslots.at[o], ss.at[5], rs.at[5], at_xy(o)))
    g2 = [remote(gz.at[zc], gz.at[zc], ss.at[6], rs.at[6], at_zc(o)) for o in range(1, 2 * nz)]
    g3 = [remote(gsum.at[mine_g, :], gsum.at[mine_g, :], ss.at[7], rs.at[7], at_xy(o)) for o in range(1, nx * ny)]

    part = at[:, columns(x)]
    g[...] = dot(part, part, ((1,), (1,)), HIGH)
    start(g1)
    arrive(2, units(2))
    start(onward[2:])

    @pl.when(root)
    def _():
        lead_a.wait()

    @pl.when(first & jnp.logical_not(root))
    def _():
        a1_to_q(1).wait_recv()

    @pl.when(first)
    def _():
        for o in range(1, nz):
            a1_to_z(o).start()

    arrive(5, gslots.at[1 : nx * ny])
    total = g[mine_g, :]
    for o in range(1, nx * ny):
        total = total + gslots[o]
    gz[zc] = total
    start(g2)

    @pl.when(jnp.logical_not(first))
    def _():
        a1_to_z(1).wait_recv()

    start(a1_gather)

    @pl.when(root)
    def _():
        lead_t.wait()

    @pl.when(first & jnp.logical_not(root))
    def _():
        t1_to_q(1).wait_recv()

    @pl.when(first)
    def _():
        for o in range(1, nz):
            t1_to_z(o).start()

    arrive(3, units(4))
    product(0)
    arrive(6, gz.at[1 : 2 * nz])
    total = gz[0]
    for o in range(1, 2 * nz):
        total = total + gz[o]
    gsum[mine_g, :] = total
    start(g3)
    arrive(4, units(3))
    product(1)
    sum_scattered(0)
    for i in range(0, at.shape[1], N):
        hi, lo = split(at[:, i : i + N].T)
        ahi_out[i : i + N, :] = hi
        alo_out[i : i + N, :] = lo
    arrive(19, a1t.at[w:N, :])
    a1 = a1t[...].T
    row = lax.broadcasted_iota(jnp.int32, (N, N), 0)
    col = lax.broadcasted_iota(jnp.int32, (N, N), 1)
    m2[0:N, :] = a1
    m2[N : 2 * N, :] = jnp.where(row == col, 1.0, 0.0)
    arrive(7, gsum.at[gpart:N, :])

    lane = lax.broadcasted_iota(jnp.int32, (8, N), 1)
    sub = lax.broadcasted_iota(jnp.int32, (8, N), 0)
    blocks = N // 8
    m1[...] = gsum[...]
    for b in range(blocks + 1):
        if b == 3:
            sum_scattered(1)
        if b == 9:
            sum_exchanged(0)
        if b == 13:
            sum_exchanged(1)
        if b == 5:

            @pl.when(jnp.logical_not(first))
            def _():
                t1_to_z(1).wait_recv()

            start(t1_gather)
        steps, pivots = [], []
        if b < blocks:
            steps.append(eliminate(m1, b, False, pivots))
        if b > 0:
            steps.append(eliminate(m2, b - 1, True, []))
        interleave(*steps)
        if b < blocks:
            rows = slice(8 * b, 8 * b + 8)
            scale = lax.rsqrt(pivots[0])
            diagonal = sub + 8 * b
            block = m1[rows, :] * scale
            upper = jnp.where(lane >= diagonal, block, 0.0)
            inverse = jnp.where(lane < diagonal, block, jnp.where(lane == diagonal, scale, 0.0))
            lead = a1[8 * b : 8 * b + 8, :]
            diag = jnp.sum(lead * inverse, axis=1, keepdims=True)
            sign = jnp.where(diag >= 0, -1.0, 1.0)
            signed = sign * upper
            r_out[rows, :] = signed
            rit[rows, :] = sign * inverse
            bmat[rows, :] = lead - signed
            m2[rows, :] = m2[rows, :] - signed
    v = jnp.where(row <= col, m2[N : 2 * N, :], 0.0)
    linv = jnp.where(row == col, 1.0, jnp.where(row > col, m2[0:N, :], 0.0))
    vt = v.T
    m1[...] = vt
    vxt_out[...] = m1[own, :]
    l1t = jnp.where(row == col, 1.0, jnp.where(row < col, dot(vt, bmat[...], ((1,), (1,)), HIGH), 0.0))
    m1[...] = l1t
    l1xt_out[...] = m1[own, :]
    inv = dot3(v, linv)
    weight = dot3(inv, rit[...])
    arrive(16, t1.at[piece:N, :])
    known = dot3(inv, t1[...])
    sent(1, units(3, 3))
    sent(5, gslots.at[1 : nx * ny])
    sent(6, gz.at[1 : 2 * nz])
    sent(7, gsum.at[gpart:N, :])
    for h in range(2):
        sent(8 + h, cslots[h].at[1:Q])
    sent(10, cz[0].at[1:nz])
    sent(16, t1.at[piece:N, :])
    sent(19, a1t.at[w:N, :])

    @pl.when(root)
    def _():
        sent(14, t1.at[piece:N, :])
        sent(17, m2.at[0 : (Q - 1) * w, :])

    @pl.when(first)
    def _():
        sent(15, t1.at[0 : (nz - 1) * piece, :])
        sent(18, m2.at[0 : (nz - 1) * w, :])

    arrive(12, call[0].at[1:Q])
    collect(0)
    sent(11, cz[1].at[1:nz])
    arrive(13, call[1].at[1:Q])
    collect(1)
    chi, clo = split(csum[...])
    both = jnp.concatenate([weight, rit[...]], axis=0)
    bhi, blo = split(both)
    both = dot(bhi, chi) + (dot(bhi, clo) + dot(blo, chi))
    khi, klo = split(known - both[:N])
    khi_out[...] = khi
    klo_out[...] = klo
    d_out[...] = both[N:]
    for h in range(2):
        sent(12 + h, call[h].at[1:Q])


def update_kernel(
    t_ref, ahi_ref, alo_ref, khi_ref, klo_ref, d_ref, vxt_ref, l1xt_ref, r_ref, out_ref, yt_ref, factor_ref, buf, yt, sems
):
    root = lax.axis_index("row") == 0
    nt = ((1,), (1,))
    rows = t_ref.shape[0]
    copies = [pltpu.make_async_copy(r_ref, factor_ref, sems.at[0])]
    copies[0].start()
    khi, klo = khi_ref[...], klo_ref[...]
    k2 = jnp.concatenate([khi, khi], axis=0)
    chunk = 256
    for i in range(rows // chunk):
        part = slice(i * chunk, (i + 1) * chunk)
        ahi, alo = ahi_ref[part, :], alo_ref[part, :]
        a2 = jnp.concatenate([ahi, alo], axis=1)
        buf[part, :] = t_ref[part, :] - (dot(a2, k2) + dot(ahi, klo))
        if i == 0:

            @pl.when(root)
            def _():
                buf[0:N, :] = d_ref[...]

        copies.append(pltpu.make_async_copy(buf.at[part, :], out_ref.at[part, :], sems.at[i + 1]))
        copies[-1].start()
        if i == rows // chunk - 3:
            vhi, vlo = split(vxt_ref[...])
            ahi, alo = ahi_ref[...], alo_ref[...]
            yt[...] = dot(vhi, ahi, nt) + dot(vhi, alo, nt) + dot(vlo, ahi, nt)

            @pl.when(root)
            def _():
                yt[:, 0:N] = l1xt_ref[...]

            copies.append(pltpu.make_async_copy(yt, yt_ref, sems.at[rows // chunk + 1]))
            copies[-1].start()
    for copy in copies:
        copy.wait()


def per_device(nz, nx, panel_block, trailing):
    rows, cols = trailing.shape
    w = N // nx
    dma = pltpu.SemaphoreType.DMA
    any_spec = pl.BlockSpec(memory_space=pltpu.HBM)
    vmem = pl.BlockSpec(memory_space=pltpu.VMEM)
    hbm = functools.partial(pltpu.with_memory_space_constraint, memory_space=pltpu.HBM)
    shape = jax.ShapeDtypeStruct
    ahi, alo, khi, klo, d, vxt, l1xt, factor, held = pl.pallas_call(
        functools.partial(factor_kernel, nz, nx),
        out_shape=[
            shape((rows, N), BF16), shape((rows, N), BF16), shape((N, cols), BF16), shape((N, cols), BF16), shape((N, cols), F32),
            shape((w, N), F32), shape((w, N), F32), shape((N, N), F32), shape((rows, cols), F32),
        ],
        in_specs=[any_spec, any_spec],
        out_specs=[vmem] * 9,
        scratch_shapes=[
            pltpu.VMEM((N, rows), F32), pltpu.VMEM((rows, cols), BF16),
            pltpu.VMEM((rows, cols), BF16), pltpu.VMEM((N, N), F32), pltpu.VMEM((N, cols), F32),
            pltpu.VMEM((N, N), F32), pltpu.VMEM((16, 8, N), F32), pltpu.VMEM((2 * nz, 8, N), F32), pltpu.VMEM((N, N), F32),
            pltpu.VMEM((3 * w, cols), F32), pltpu.VMEM((N, cols), F32),
            pltpu.VMEM((N, N), F32), pltpu.VMEM((2 * N, N), F32), pltpu.VMEM((N, N), F32), pltpu.VMEM((N, N), F32),
        ] + [pltpu.VMEM((count, w * wide // Q, cols), F32) for count in (Q, Q, nz, Q) for wide in (3, 1)] + [
            dma((4,)), dma((20,)), dma((20,)),
        ],
        compiler_params=pltpu.CompilerParams(
            collective_id=0, has_side_effects=True, vmem_limit_bytes=48 * 1024 * 1024
        ),
        name="factor",
    )(hbm(panel_block.T), hbm(trailing))
    updated, yt, factor = pl.pallas_call(
        update_kernel,
        out_shape=[shape((rows, cols), F32), shape((w, rows), F32), shape((N, N), F32)],
        in_specs=[vmem] * 9,
        out_specs=[any_spec] * 3,
        scratch_shapes=[pltpu.VMEM((rows, cols), F32), pltpu.VMEM((w, rows), F32), dma((rows // 256 + 2,))],
        compiler_params=pltpu.CompilerParams(vmem_limit_bytes=32 * 1024 * 1024),
        name="update",
    )(held, ahi, alo, khi, klo, d, vxt, l1xt, factor)
    return updated, yt.T, factor


def solution(mesh):
    nz, nx = mesh.shape["row"] // Q, mesh.shape["col"]
    in_specs = (P("row", "col"), P("row", "col"))
    out_specs = (P("row", "col"), P("row", "col"), P())
    return jax.shard_map(
        functools.partial(per_device, nz, nx), mesh=mesh, in_specs=in_specs, out_specs=out_specs, check_vma=False
    )
```

```python
import functools

import jax
import jax.numpy as jnp
from jax import lax
from jax.experimental import pallas as pl
from jax.experimental.pallas import tpu as pltpu
from jax.sharding import PartitionSpec as P

F32 = jnp.float32
BF16 = jnp.bfloat16
HIGH = lax.Precision.HIGHEST
N = 128
Q = 8


def dot(a, b, dims=((1,), (0,)), precision=None):
    return lax.dot_general(a, b, (dims, ((), ())), precision=precision, preferred_element_type=F32)


def split(x):
    hi = x.astype(BF16)
    return hi, (x - hi.astype(F32)).astype(BF16)


def dot3(a, b):
    (ah, al), (bh, bl) = split(a), split(b)
    return dot(ah, bh) + (dot(ah, bl) + dot(al, bh))


def eliminate(m_ref, b, bottom, out):
    r0 = 8 * b
    lane = lax.broadcasted_iota(jnp.int32, (8, N), 1)
    sub = lax.broadcasted_iota(jnp.int32, (8, N), 0)
    parts = []
    if r0 + 8 < N:
        parts.append((r0 + 8, N - r0 - 8, False))
    if bottom:
        parts.append((N, r0 + 8, True))
    rows = m_ref[r0 : r0 + 8, :]
    rest = [m_ref[s : s + n, :] for s, n, _ in parts]
    cols = [
        [jnp.broadcast_to(p[:, r0 + j : r0 + j + 1], (p.shape[0], N)) for j in range(8)]
        for p in [rows] + rest
    ]
    mults, pivots = [], None
    for k in range(8):
        yield
        c0 = cols[0][k]
        d = jnp.broadcast_to(c0[k : k + 1, :], (8, N))
        inv = 1.0 / d
        pivots = d if pivots is None else jnp.where(sub == k, d, pivots)
        ms = [jnp.where(sub > k, c0 * inv, 0.0)] + [c[k] * inv[0:1, :] for c in cols[1:]]
        mults.append(ms)
        for j in range(k + 1, 8):
            top = cols[0][j][k : k + 1, :]
            for i in range(len(cols)):
                cols[i][j] = cols[i][j] - ms[i] * top
    pivot_rows = []
    for k in range(8):
        lk = r0 + k
        row = jnp.where(lane[0:1] == lk, 1.0, rows[k : k + 1, :])
        rows = jnp.where((lane == lk) & (sub > k), 0.0, rows) - mults[k][0] * row
        pivot_rows.append(jnp.where((lane[0:1] > lk) & (lane[0:1] < r0 + 8), 0.0, row))
    for i, (s, n, low) in enumerate(parts):
        lane_n = lax.broadcasted_iota(jnp.int32, (n, N), 1)
        acc = jnp.where((lane_n >= r0) & (lane_n < r0 + 8), 0.0, rest[i])
        for k in range(8):
            row = jnp.where(lane[0:1] >= r0 + 8, pivot_rows[k], 0.0) if low else pivot_rows[k]
            acc = acc - mults[k][i + 1] * row
        if low:
            for k in range(8):
                acc = jnp.where(lane_n == r0 + k, mults[k][i + 1], acc)
        m_ref[s : s + n, :] = acc
    m_ref[r0 : r0 + 8, :] = rows
    out.append(pivots)


def interleave(*steps):
    steps = list(steps)
    while steps:
        for step in list(steps):
            if next(step, True) is True:
                steps.remove(step)


def remote(src, dst, send, recv, device):
    return pltpu.make_async_remote_copy(
        src_ref=src, dst_ref=dst, send_sem=send, recv_sem=recv, device_id=device, device_id_type=pl.DeviceIdType.MESH
    )


def factor_kernel(
    nz, nx,
    pt_ref, t_ref,
    ahi_out, alo_out, khi_out, klo_out, d_out, vxt_out, l1xt_out, r_out, t,
    at, thi, tlo, a1t, t1, g, gslots, gz, gsum, strips, csum, m1, m2, rit, bmat, p0, p1, s0, s1, z0, z1, e0, e1,
    load_sem, ss, rs,
):
    cparts, cslots, cz, call = (p0, p1), (s0, s1), (z0, z1), (e0, e1)
    r = lax.axis_index("row")
    x = lax.axis_index("col")
    z, q = lax.div(r, Q), lax.rem(r, Q)
    ny = Q // 2
    y, core = lax.div(q, 2), lax.rem(q, 2)
    w = N // nx
    seg = pt_ref.shape[1] // nx

    def along_x(o):
        return lax.rem(x + o, nx)

    def along_y(o):
        return lax.rem(y + o, ny)

    def at_x(o):
        return {"col": along_x(o)}

    def at_q(o):
        return {"row": z * Q + lax.rem(q + o, Q)}

    def at_z(o):
        return {"row": lax.rem(z + o, nz) * Q + q}

    def at_xy(o):
        return {"row": z * Q + along_y(o % ny) * 2 + core, "col": along_x(o // ny)}

    def at_zc(o):
        return {"row": lax.rem(z + o // 2, nz) * Q + y * 2 + lax.rem(core + o % 2, 2)}

    load_t = pltpu.make_async_copy(t_ref, t, load_sem.at[0])
    load_t.start()
    own = pl.ds(pl.multiple_of(x * w, w), w)
    load_a = pltpu.make_async_copy(pt_ref, at.at[own, :], load_sem.at[1])
    load_a.start()

    barrier = pltpu.get_barrier_semaphore()
    greeted = [at_xy(o) for o in range(1, nx * ny)] + [at_zc(o) for o in range(1, 2 * nz)]
    greeted += [{"row": z * Q + along_y(o) * 2 + (1 - core)} for o in range(1, ny)]
    for device in greeted:
        pl.semaphore_signal(barrier, inc=1, device_id=device, device_id_type=pl.DeviceIdType.MESH)
    pl.semaphore_wait(barrier, len(greeted))

    def columns(s):
        return pl.ds(pl.multiple_of(s * seg, seg), seg)

    def strip(owner, cols):
        return at.at[pl.ds(pl.multiple_of(owner * w, w), w), cols]

    def tell(send, recv, o, s):
        return remote(pt_ref.at[:, columns(s)], strip(x, columns(s)), ss.at[send], rs.at[recv], at_x(o))

    def forward(o, owner, cols):
        return remote(strip(owner, cols), strip(owner, cols), ss.at[1], rs.at[4], at_x(o))

    def whole(i, ref, recv=None):
        return remote(ref, ref, ss.at[i], rs.at[i if recv is None else recv], at_x(1))

    xp, xm, x2 = along_x(1), along_x(nx - 1), along_x(2)
    plus, minus = 1, nx - 1
    first_half = pl.ds(pl.multiple_of(xm * seg, seg), seg // 2)
    second_half = pl.ds(pl.multiple_of(xp * seg + seg // 2, seg // 2), seg // 2)
    near_first = [tell(0, 0, plus, xp), tell(0, 0, minus, xm), tell(0, 1, 2, x2)]
    near_rest = [
        tell(1, 2, plus, x), tell(1, 2, minus, x),
        tell(1, 3, plus, x2), tell(1, 3, minus, x2), tell(1, 3, plus, xm), tell(1, 3, minus, xp),
    ]
    onward = [
        forward(plus, xm, columns(x)), forward(minus, xp, columns(x)),
        forward(plus, xm, first_half), forward(minus, xp, second_half),
    ]

    def units(n, m=1):
        return at.at[0 : n * w, 0 : m * seg]

    def start(copies):
        for copy in copies:
            copy.start()

    def arrive(i, ref):
        whole(i, ref, i).wait_recv()

    def sent(i, ref):
        whole(i, ref).wait_send()

    start(near_first)

    owners = [[x, xp, xm], [x2]]
    c1, c2, c3 = [], [], []
    for h in range(2):
        c1.append([
            remote(cparts[h].at[lax.rem(q + o, Q)], cslots[h].at[o], ss.at[8 + h], rs.at[8 + h], at_q(o))
            for o in range(1, Q)
        ])
        c2.append([remote(cz[h].at[z], cz[h].at[z], ss.at[10 + h], rs.at[10 + h], at_z(o)) for o in range(1, nz)])
        c3.append([remote(call[h].at[q], call[h].at[q], ss.at[12 + h], rs.at[12 + h], at_q(o)) for o in range(1, Q)])

    def product(h):
        rows = len(owners[h]) * w
        n = rows // Q
        pieces = [split(at[pl.ds(pl.multiple_of(owner * w, w), w), :]) for owner in owners[h]]
        hi = jnp.concatenate([p[0] for p in pieces], axis=0)
        lo = jnp.concatenate([p[1] for p in pieces], axis=0)
        both = dot(jnp.concatenate([hi, lo], axis=0), thi[...])
        strips[0:rows, :] = both[:rows] + both[rows:] + dot(hi, tlo[...])
        for j in range(Q):
            cparts[h][j] = strips[j * n : (j + 1) * n, :]
        start(c1[h])

    def sum_scattered(h):
        arrive(8 + h, cslots[h].at[1:Q])
        total = cparts[h][q]
        for o in range(1, Q):
            total = total + cslots[h][o]
        cz[h][z] = total
        start(c2[h])

    def sum_exchanged(h):
        arrive(10 + h, cz[h].at[1:nz])
        total = cz[h][0]
        for o in range(1, nz):
            total = total + cz[h][o]
        call[h][q] = total
        start(c3[h])

    def collect(h):
        n = len(owners[h]) * w // Q
        for j in range(Q):
            strips[j * n : (j + 1) * n, :] = call[h][j]
        for i, owner in enumerate(owners[h]):
            csum[pl.ds(pl.multiple_of(owner * w, w), w), :] = strips[i * w : (i + 1) * w, :]

    root = r == 0
    first = z == 0
    piece = N // Q
    mine_piece = pl.ds(pl.multiple_of(q * piece, piece), piece)
    lead_cols = pl.ds(0, N)

    def t1_to_q(o):
        rows = pl.ds(pl.multiple_of(lax.rem(q + o, Q) * piece, piece), piece)
        return remote(t_ref.at[rows, :], t1.at[rows, :], ss.at[14], rs.at[14], at_q(o))

    def a1_to_q(o):
        return remote(pt_ref.at[:, lead_cols], a1t.at[own, :], ss.at[17], rs.at[17], at_q(o))

    def t1_to_z(o):
        return remote(t1.at[mine_piece, :], t1.at[mine_piece, :], ss.at[15], rs.at[15], at_z(o))

    def a1_to_z(o):
        return remote(a1t.at[own, :], a1t.at[own, :], ss.at[18], rs.at[18], at_z(o))

    t1_gather = [
        remote(t1.at[mine_piece, :], t1.at[mine_piece, :], ss.at[16], rs.at[16], at_q(o)) for o in range(1, Q)
    ]
    a1_gather = [remote(a1t.at[own, :], a1t.at[own, :], ss.at[19], rs.at[19], at_x(o)) for o in range(1, nx)]
    lead_t = pltpu.make_async_copy(t_ref.at[mine_piece, :], t1.at[mine_piece, :], load_sem.at[2])
    lead_a = pltpu.make_async_copy(pt_ref.at[:, lead_cols], a1t.at[own, :], load_sem.at[3])

    @pl.when(root)
    def _():
        for o in range(1, Q):
            a1_to_q(o).start()
        lead_a.start()
        lead_t.start()
        for o in range(1, Q):
            t1_to_q(o).start()

    load_t.wait()
    thi[...] = t[...].astype(BF16)
    tlo[...] = (t[...] - thi[...].astype(F32)).astype(BF16)
    load_a.wait()

    start(near_rest)
    arrive(0, units(2))
    start(onward[:2])
    arrive(1, units(1))

    gp = x * ny + y
    gpart = N // (nx * ny)
    mine_g = pl.ds(pl.multiple_of(gp * gpart, gpart), gpart)
    zc = z * 2 + core
    g1 = []
    for o in range(1, nx * ny):
        there = pl.multiple_of((along_x(o // ny) * ny + along_y(o % ny)) * gpart, gpart)
        g1.append(remote(g.at[pl.ds(there, gpart), :], gslots.at[o], ss.at[5], rs.at[5], at_xy(o)))
    g2 = [remote(gz.at[zc], gz.at[zc], ss.at[6], rs.at[6], at_zc(o)) for o in range(1, 2 * nz)]
    g3 = [remote(gsum.at[mine_g, :], gsum.at[mine_g, :], ss.at[7], rs.at[7], at_xy(o)) for o in range(1, nx * ny)]

    part = at[:, columns(x)]
    g[...] = dot(part, part, ((1,), (1,)), HIGH)
    start(g1)
    arrive(2, units(2))
    start(onward[2:])

    @pl.when(root)
    def _():
        lead_a.wait()

    @pl.when(first & jnp.logical_not(root))
    def _():
        a1_to_q(1).wait_recv()

    @pl.when(first)
    def _():
        for o in range(1, nz):
            a1_to_z(o).start()

    arrive(5, gslots.at[1 : nx * ny])
    total = g[mine_g, :]
    for o in range(1, nx * ny):
        total = total + gslots[o]
    gz[zc] = total
    start(g2)

    @pl.when(jnp.logical_not(first))
    def _():
        a1_to_z(1).wait_recv()

    start(a1_gather)

    @pl.when(root)
    def _():
        lead_t.wait()

    @pl.when(first & jnp.logical_not(root))
    def _():
        t1_to_q(1).wait_recv()

    @pl.when(first)
    def _():
        for o in range(1, nz):
            t1_to_z(o).start()

    arrive(3, units(4))
    product(0)
    arrive(6, gz.at[1 : 2 * nz])
    total = gz[0]
    for o in range(1, 2 * nz):
        total = total + gz[o]
    gsum[mine_g, :] = total
    start(g3)
    arrive(4, units(3))
    product(1)
    sum_scattered(0)
    for i in range(0, at.shape[1], N):
        hi, lo = split(at[:, i : i + N].T)
        ahi_out[i : i + N, :] = hi
        alo_out[i : i + N, :] = lo
    arrive(19, a1t.at[w:N, :])
    a1 = a1t[...].T
    row = lax.broadcasted_iota(jnp.int32, (N, N), 0)
    col = lax.broadcasted_iota(jnp.int32, (N, N), 1)
    m2[0:N, :] = a1
    m2[N : 2 * N, :] = jnp.where(row == col, 1.0, 0.0)
    arrive(7, gsum.at[gpart:N, :])

    lane = lax.broadcasted_iota(jnp.int32, (8, N), 1)
    sub = lax.broadcasted_iota(jnp.int32, (8, N), 0)
    blocks = N // 8
    m1[...] = gsum[...]
    for b in range(blocks + 1):
        if b == 4:
            sum_scattered(1)
        if b == 11:
            sum_exchanged(0)
        if b == 15:
            sum_exchanged(1)
        if b == 2:

            @pl.when(jnp.logical_not(first))
            def _():
                t1_to_z(1).wait_recv()

            start(t1_gather)
        steps, pivots = [], []
        if b < blocks:
            steps.append(eliminate(m1, b, False, pivots))
        if b > 0:
            steps.append(eliminate(m2, b - 1, True, []))
        interleave(*steps)
        if b < blocks:
            rows = slice(8 * b, 8 * b + 8)
            scale = lax.rsqrt(pivots[0])
            diagonal = sub + 8 * b
            block = m1[rows, :] * scale
            upper = jnp.where(lane >= diagonal, block, 0.0)
            inverse = jnp.where(lane < diagonal, block, jnp.where(lane == diagonal, scale, 0.0))
            lead = a1[8 * b : 8 * b + 8, :]
            diag = jnp.sum(lead * inverse, axis=1, keepdims=True)
            sign = jnp.where(diag >= 0, -1.0, 1.0)
            signed = sign * upper
            r_out[rows, :] = signed
            rit[rows, :] = sign * inverse
            bmat[rows, :] = lead - signed
            m2[rows, :] = m2[rows, :] - signed
    v = jnp.where(row <= col, m2[N : 2 * N, :], 0.0)
    linv = jnp.where(row == col, 1.0, jnp.where(row > col, m2[0:N, :], 0.0))
    vt = v.T
    m1[...] = vt
    vxt_out[...] = m1[own, :]
    l1t = jnp.where(row == col, 1.0, jnp.where(row < col, dot(vt, bmat[...], ((1,), (1,)), HIGH), 0.0))
    m1[...] = l1t
    l1xt_out[...] = m1[own, :]
    inv = dot3(v, linv)
    weight = dot3(inv, rit[...])
    arrive(16, t1.at[piece:N, :])
    known = dot3(inv, t1[...])
    sent(0, units(3))
    sent(1, units(3, 3))
    sent(5, gslots.at[1 : nx * ny])
    sent(6, gz.at[1 : 2 * nz])
    sent(7, gsum.at[gpart:N, :])
    for h in range(2):
        sent(8 + h, cslots[h].at[1:Q])
    sent(10, cz[0].at[1:nz])
    sent(16, t1.at[piece:N, :])
    sent(19, a1t.at[w:N, :])

    @pl.when(root)
    def _():
        sent(14, t1.at[piece:N, :])
        sent(17, m2.at[0 : (Q - 1) * w, :])

    @pl.when(first)
    def _():
        sent(15, t1.at[0 : (nz - 1) * piece, :])
        sent(18, m2.at[0 : (nz - 1) * w, :])

    arrive(12, call[0].at[1:Q])
    collect(0)
    sent(11, cz[1].at[1:nz])
    arrive(13, call[1].at[1:Q])
    collect(1)
    chi, clo = split(csum[...])
    both = jnp.concatenate([weight, rit[...]], axis=0)
    bhi, blo = split(both)
    both = dot(bhi, chi) + (dot(bhi, clo) + dot(blo, chi))
    khi, klo = split(known - both[:N])
    khi_out[...] = khi
    klo_out[...] = klo
    d_out[...] = both[N:]
    for h in range(2):
        sent(12 + h, call[h].at[1:Q])


def update_kernel(
    t_ref, ahi_ref, alo_ref, khi_ref, klo_ref, d_ref, vxt_ref, l1xt_ref, r_ref, out_ref, yt_ref, factor_ref, buf, yt, sems
):
    root = lax.axis_index("row") == 0
    nt = ((1,), (1,))
    rows = t_ref.shape[0]
    copies = [pltpu.make_async_copy(r_ref, factor_ref, sems.at[0])]
    copies[0].start()
    khi, klo = khi_ref[...], klo_ref[...]
    k2 = jnp.concatenate([khi, khi], axis=0)
    chunk = 256
    for i in range(rows // chunk):
        part = slice(i * chunk, (i + 1) * chunk)
        ahi, alo = ahi_ref[part, :], alo_ref[part, :]
        a2 = jnp.concatenate([ahi, alo], axis=1)
        buf[part, :] = t_ref[part, :] - (dot(a2, k2) + dot(ahi, klo))
        if i == 0:

            @pl.when(root)
            def _():
                buf[0:N, :] = d_ref[...]

        copies.append(pltpu.make_async_copy(buf.at[part, :], out_ref.at[part, :], sems.at[i + 1]))
        copies[-1].start()
        if i == rows // chunk - 3:
            vhi, vlo = split(vxt_ref[...])
            ahi, alo = ahi_ref[...], alo_ref[...]
            yt[...] = dot(vhi, ahi, nt) + dot(vhi, alo, nt) + dot(vlo, ahi, nt)

            @pl.when(root)
            def _():
                yt[:, 0:N] = l1xt_ref[...]

            copies.append(pltpu.make_async_copy(yt, yt_ref, sems.at[rows // chunk + 1]))
            copies[-1].start()
    for copy in copies:
        copy.wait()


def per_device(nz, nx, panel_block, trailing):
    rows, cols = trailing.shape
    w = N // nx
    dma = pltpu.SemaphoreType.DMA
    any_spec = pl.BlockSpec(memory_space=pltpu.HBM)
    vmem = pl.BlockSpec(memory_space=pltpu.VMEM)
    hbm = functools.partial(pltpu.with_memory_space_constraint, memory_space=pltpu.HBM)
    shape = jax.ShapeDtypeStruct
    ahi, alo, khi, klo, d, vxt, l1xt, factor, held = pl.pallas_call(
        functools.partial(factor_kernel, nz, nx),
        out_shape=[
            shape((rows, N), BF16), shape((rows, N), BF16), shape((N, cols), BF16), shape((N, cols), BF16), shape((N, cols), F32),
            shape((w, N), F32), shape((w, N), F32), shape((N, N), F32), shape((rows, cols), F32),
        ],
        in_specs=[any_spec, any_spec],
        out_specs=[vmem] * 9,
        scratch_shapes=[
            pltpu.VMEM((N, rows), F32), pltpu.VMEM((rows, cols), BF16),
            pltpu.VMEM((rows, cols), BF16), pltpu.VMEM((N, N), F32), pltpu.VMEM((N, cols), F32),
            pltpu.VMEM((N, N), F32), pltpu.VMEM((16, 8, N), F32), pltpu.VMEM((2 * nz, 8, N), F32), pltpu.VMEM((N, N), F32),
            pltpu.VMEM((3 * w, cols), F32), pltpu.VMEM((N, cols), F32),
            pltpu.VMEM((N, N), F32), pltpu.VMEM((2 * N, N), F32), pltpu.VMEM((N, N), F32), pltpu.VMEM((N, N), F32),
        ] + [pltpu.VMEM((count, w * wide // Q, cols), F32) for count in (Q, Q, nz, Q) for wide in (3, 1)] + [
            dma((4,)), dma((20,)), dma((20,)),
        ],
        compiler_params=pltpu.CompilerParams(
            collective_id=0, has_side_effects=True, vmem_limit_bytes=48 * 1024 * 1024
        ),
        name="factor",
    )(hbm(panel_block.T), hbm(trailing))
    updated, yt, factor = pl.pallas_call(
        update_kernel,
        out_shape=[shape((rows, cols), F32), shape((w, rows), F32), shape((N, N), F32)],
        in_specs=[vmem] * 9,
        out_specs=[any_spec] * 3,
        scratch_shapes=[pltpu.VMEM((rows, cols), F32), pltpu.VMEM((w, rows), F32), dma((rows // 256 + 2,))],
        compiler_params=pltpu.CompilerParams(vmem_limit_bytes=32 * 1024 * 1024),
        name="update",
    )(held, ahi, alo, khi, klo, d, vxt, l1xt, factor)
    return updated, yt.T, factor


def solution(mesh):
    nz, nx = mesh.shape["row"] // Q, mesh.shape["col"]
    in_specs = (P("row", "col"), P("row", "col"))
    out_specs = (P("row", "col"), P("row", "col"), P())
    return jax.shard_map(
        functools.partial(per_device, nz, nx), mesh=mesh, in_specs=in_specs, out_specs=out_specs, check_vma=False
    )
```
